512 devices in a mesh: prompt: 32 (over y_lo, x, core), ctx: 16 (over z, y_hi).
Axes of the slice: x: 4, y: 8 (y_hi: 2, y_lo: 4; y = y_hi * 4 + y_lo), z: 8, core: 2. Of those that a mesh axis runs over, the one named last changes fastest.
Arguments:
- prefix_qkv: bfloat16 [32, 2048, 768], P('prompt', 'ctx'), may hold values from -8 to 8
- rollout: bfloat16 [32, 16, 32, 32, 768], P('prompt', 'ctx'), may hold values from -8 to 8
- arrival_order: int32 [32, 16, 1024], P('prompt', 'ctx'), may hold values from 0 to 1023, each once within a row
- resp_len: int32 [32, 32], P('prompt', 'ctx'), may hold values from 1 to 512, 10240 in all within a row
Outputs:
- prefix_out: bfloat16 [32, 2048, 512], P('prompt', 'ctx')
- resp_out: bfloat16 [32, 32, 512, 512], P('prompt', 'ctx')
The draws below stay inside these ranges and needn't reach their ends.
All inputs are finite; a program needn't handle non-finite values. No bound on the sum of `resp_len` on one device may be relied on, other than what follows from the above.
Results may differ from the reference program's by a relative error of at most 0.0075.
Values may be sent and summed in bfloat16 or wider, within the bound.
A program may use at most 64 MiB of HBM per device.

```python
import math
import jax
import jax.numpy as jnp
import numpy as np
from jax import lax

HEAD = 128
HEADS = 4
SLOT = 512
RESP_DEV = 2
PREFIX = 2048
RESPONSES = 32
FEAT = 768
ROWS_PEER = 32
N_PROMPT = 32
N_CTX = 16


def draw_prefix_qkv(key, part):
    array_shape = (N_PROMPT, PREFIX, (HEADS + 2) * HEAD)
    return jax.random.truncated_normal(jax.random.fold_in(key, 2), -6.0, 6.0, array_shape, jnp.float32).astype(jnp.bfloat16)


def draw_rollout(key, part):
    array_shape = (N_PROMPT, N_CTX, N_PROMPT, ROWS_PEER, (HEADS + 2) * HEAD)
    return jax.random.truncated_normal(jax.random.fold_in(key, 4), -6.0, 6.0, array_shape, jnp.float32).astype(jnp.bfloat16)


def length_profile(amount, total, reach, lean):
    loads = [(1 << 20) // math.isqrt(rank ** lean) + 1 for rank in range(2, amount + 1)]
    rest, holding = total - reach - (amount - 1), [1] * (amount - 1)
    while rest > 0:
        movable = [i for i in range(amount - 1) if holding[i] < reach]
        mass, left = sum([loads[i] for i in movable]), rest
        for i in movable:
            extra = min(reach - holding[i], max(1, left * loads[i] // mass), rest)
            holding[i] = holding[i] + extra
            rest = rest - extra
    return np.array([reach] + holding)


def ragged_sizes(rng, amount, total, bound, skew):
    if amount == 2:
        one = jax.random.randint(rng, (), max(1, total - bound), min(bound, total - 1) + 1)
        return jnp.stack([one, total - one])
    sizes = jnp.asarray(length_profile(amount, total, bound, skew), jnp.int32)
    pairs = (amount - 1) // 2
    giver, sink = sizes[1:1 + 2 * pairs:2], sizes[2:2 + 2 * pairs:2]
    slack = jnp.minimum(giver - 1, bound - sink)
    shifted = jax.random.randint(jax.random.fold_in(rng, 1), (pairs,), 0, 1 << 20) % (slack + 1)
    sizes = sizes.at[1:1 + 2 * pairs:2].set(giver - shifted).at[2:2 + 2 * pairs:2].set(sink + shifted)
    return sizes[jax.random.permutation(jax.random.fold_in(rng, 2), amount)]


def setup_inputs(seed: int = 0) -> dict:
    arg_keys = jax.random.split(jax.random.key(seed), 5)
    return {
        "prefix_qkv": draw_prefix_qkv(jax.random.fold_in(arg_keys[4], 71), 0),
        "rollout": draw_rollout(jax.random.fold_in(arg_keys[4], 71), 0),
        "arrival_order": jax.vmap(lambda own: jax.random.permutation(own, RESP_DEV * SLOT))(jax.random.split(arg_keys[2], N_PROMPT * N_CTX)).reshape((N_PROMPT, N_CTX, RESP_DEV * SLOT)).astype(jnp.int32),
        "resp_len": jax.vmap(lambda own: ragged_sizes(own, RESPONSES, N_CTX * RESP_DEV * 5 // 8 * SLOT, SLOT, 2))(jax.random.split(arg_keys[3], N_PROMPT)).reshape((N_PROMPT, RESPONSES)).astype(jnp.int32),
    }


MASKED_SCORE = -1e30


def attend(queries, key_rows, values, allowed):
    row_count = queries.shape[0]
    head_size = key_rows.shape[1]
    head_count = queries.shape[1] // head_size
    q_heads = queries.reshape(row_count, head_count, head_size).astype(jnp.float32)
    scores = jnp.einsum("rhd,kd->hrk", q_heads, key_rows.astype(jnp.float32)) * (head_size ** -0.5)
    scores = jnp.where(allowed[None], scores, MASKED_SCORE)
    row_max = jnp.max(scores, axis=-1, keepdims=True)
    weights = jnp.exp(scores - row_max)
    row_sum = jnp.sum(weights, axis=-1)
    rounded = lax.optimization_barrier(weights.astype(jnp.bfloat16)).astype(jnp.float32)
    weighted = jnp.einsum("hrk,kd->hrd", rounded, values.astype(jnp.float32)) / row_sum[..., None]
    return jnp.transpose(weighted, (1, 0, 2)).reshape(row_count, head_count * head_size)


def reference(prefix_qkv, rollout, arrival_order, resp_len):
    query_span = HEADS * HEAD
    positions = jnp.arange(PREFIX)
    causal = positions[None, :] <= positions[:, None]
    own_pos = jnp.arange(SLOT)
    own_causal = own_pos[None, :] <= own_pos[:, None]
    full_mask = jnp.ones((SLOT, PREFIX), dtype=bool)
    response_mask = jnp.concatenate([full_mask, own_causal], axis=1)

    def one_prompt(prompt_item):
        prompt_index, prefix, row_order, lengths = prompt_item
        prefix_keys = prefix[:, query_span:query_span + HEAD]
        prefix_values = prefix[:, query_span + HEAD:]
        prefix_part = attend(prefix[:, :query_span], prefix_keys, prefix_values, causal).astype(jnp.bfloat16)
        sent_rows = jnp.take(rollout, prompt_index, axis=2)
        received = jnp.transpose(sent_rows, (1, 0, 2, 3)).reshape(N_CTX, RESP_DEV * SLOT, FEAT)
        placed = jax.vmap(lambda block_rows, block_order: jnp.take(block_rows, block_order, axis=0))(received, row_order)
        placed = placed.reshape(RESPONSES, SLOT, FEAT)

        def one_response(resp_item):
            resp_rows, resp_length = resp_item
            all_keys = jnp.concatenate([prefix_keys, resp_rows[:, query_span:query_span + HEAD]], axis=0)
            all_values = jnp.concatenate([prefix_values, resp_rows[:, query_span + HEAD:]], axis=0)
            weighted = attend(resp_rows[:, :query_span], all_keys, all_values, response_mask)
            live_rows = (own_pos < resp_length)[:, None]
            return jnp.where(live_rows, weighted, 0.0).astype(jnp.bfloat16)

        resp_part = lax.map(one_response, (placed, lengths))
        return prefix_part, resp_part

    prefix_out, resp_out = lax.map(one_prompt, (jnp.arange(N_PROMPT, dtype=jnp.int32), prefix_qkv, arrival_order, resp_len))
    return (prefix_out, resp_out)
```

```python
import functools
import math

import jax
import jax.numpy as jnp
from jax import lax
from jax.experimental import pallas as pl
from jax.experimental.pallas import tpu as pltpu
from jax.sharding import PartitionSpec as P

HEAD = 128
MASKED = -1e30
MESH = pl.DeviceIdType.MESH
SCALE2 = HEAD ** (-0.5) * math.log2(math.e)
KEY_TILE = 512


def bit_flips(index, bits):
    return [(1 - 2 * lax.rem(lax.div(index, 1 << b), 2)) * (1 << b) for b in range(bits)]


def flipped(index, flips, mask):
    for b, step in enumerate(flips):
        if mask >> b & 1:
            index = index + step
    return index


def attend_rows(queries, kt, va, s_ref, row0, keys, extra):
    rows = queries.shape[0]
    top = None
    for k0 in range(0, keys, KEY_TILE):
        s = jnp.dot(queries, kt[:, k0 : k0 + KEY_TILE], preferred_element_type=jnp.float32)
        s = extra(k0, s)
        s_ref[row0 : row0 + rows, k0 : k0 + KEY_TILE] = s
        for l0 in range(0, KEY_TILE, 128):
            part = s[:, l0 : l0 + 128]
            top = part if top is None else jnp.maximum(top, part)
    top = jnp.max(top, axis=-1, keepdims=True)
    total = None
    for k0 in range(0, keys, KEY_TILE):
        s = s_ref[row0 : row0 + rows, k0 : k0 + KEY_TILE]
        weights = jnp.exp2((s - top) * SCALE2).astype(jnp.bfloat16)
        part = jnp.dot(weights, va[k0 : k0 + KEY_TILE, :], preferred_element_type=jnp.float32)
        total = part if total is None else total + part
    return (total[:, :HEAD] / total[:, HEAD:]).astype(jnp.bfloat16)


def gather_attend(
    n_prompt, n_ctx, heads,
    prefix_ref, rollout_ref, order_ref, pout_ref, rout_ref,
    pkv, rkv, rq, pq, kt, va, s_ref, bias_ref, gcol, grow,
    local_sem, part_send, part_recv, own_send, own_recv, fwd_send, fwd_recv,
    kv_send, kv_recv, q_send, q_recv,
):
    p = lax.axis_index("prompt")
    c = lax.axis_index("ctx")
    span = heads * HEAD
    width = span + 2 * HEAD
    peers = n_prompt.bit_length() - 1
    flips = bit_flips(p, peers)
    ring = n_ctx // 2
    z, side = lax.div(c, 2), lax.rem(c, 2)
    partner = c + 1 - 2 * side
    rows_peer = rkv.shape[1]
    block = pkv.shape[1]
    prefix_keys = n_ctx * block
    own_keys = n_prompt * rows_peer

    def along(step):
        return lax.rem(z + step, ring) * 2 + side

    barrier = pltpu.get_barrier_semaphore()
    for o in range(1, n_prompt):
        pl.semaphore_signal(barrier, inc=1, device_id=(flipped(p, flips, o), c), device_id_type=MESH)
    pl.semaphore_signal(barrier, inc=1, device_id=(p, partner), device_id_type=MESH)
    for k in range(1, ring):
        pl.semaphore_signal(barrier, inc=1, device_id=(p, along(k)), device_id_type=MESH)

    own_block = prefix_ref.at[0, :, pl.ds(span, 2 * HEAD)]
    local = [
        pltpu.make_async_copy(own_block, pkv.at[c], local_sem.at[0]),
        pltpu.make_async_copy(prefix_ref.at[0, :, pl.ds(0, span)], pq, local_sem.at[1]),
        pltpu.make_async_copy(rollout_ref.at[0, 0, p, :, pl.ds(span, 2 * HEAD)], rkv.at[p], local_sem.at[2]),
        pltpu.make_async_copy(rollout_ref.at[0, 0, p, :, pl.ds(0, span)], rq.at[p], local_sem.at[3]),
    ]
    for copy in local:
        copy.start()

    def to_partner(slot):
        return pltpu.make_async_remote_copy(
            own_block, pkv.at[slot], part_send.at[0], part_recv.at[0], device_id=(p, partner), device_id_type=MESH
        )

    def own_to(k, slot):
        return pltpu.make_async_remote_copy(
            own_block, pkv.at[slot], own_send.at[k], own_recv.at[k], device_id=(p, along(k)), device_id_type=MESH
        )

    def fwd_to(k, slot):
        return pltpu.make_async_remote_copy(
            pkv.at[partner], pkv.at[slot], fwd_send.at[k], fwd_recv.at[k], device_id=(p, along(k)), device_id_type=MESH
        )

    def kv_to(o, slot):
        there = flipped(p, flips, o)
        return pltpu.make_async_remote_copy(
            rollout_ref.at[0, 0, there, :, pl.ds(span, 2 * HEAD)], rkv.at[slot],
            kv_send.at[o], kv_recv.at[o], device_id=(there, c), device_id_type=MESH,
        )

    def q_to(o, slot):
        there = flipped(p, flips, o)
        return pltpu.make_async_remote_copy(
            rollout_ref.at[0, 0, there, :, pl.ds(0, span)], rq.at[slot],
            q_send.at[o], q_recv.at[o], device_id=(there, c), device_id_type=MESH,
        )

    pl.semaphore_wait(barrier, n_prompt - 1 + 1 + ring - 1)
    half = n_prompt // 2
    to_partner(c).start()
    for k in (1, ring - 1, 2, ring - 2, 3, ring - 3, 4):
        own_to(k, c).start()
    for o in list(range(half, n_prompt)) + list(range(half // 2, half)) + list(range(1, half // 2)):
        kv_to(o, p).start()
    for o in range(1, n_prompt):
        q_to(o, p).start()

    order = order_ref[...]
    place = lax.broadcasted_iota(jnp.int32, (128, own_keys), 1).astype(jnp.float32)
    for a0 in range(0, own_keys, 128):
        arrived = lax.broadcasted_iota(jnp.int32, (128, own_keys), 0) + a0
        at = jnp.sum(jnp.where(order == arrived, place, 0.0), axis=-1, keepdims=True)
        at = jnp.broadcast_to(at, (128, 128))
        gcol[a0 : a0 + 128, :] = at
        grow[:, a0 : a0 + 128] = at.T[:8]

    va[:, HEAD:] = jnp.ones((va.shape[0], HEAD), jnp.bfloat16)
    for copy in local:
        copy.wait()

    def take_prefix(slot):
        rows = pl.ds(pl.multiple_of(slot * block, block), block)
        got = pkv[slot]
        kt[:, rows] = got[:, :HEAD].T
        va[rows, :HEAD] = got[:, HEAD:]

    take_prefix(c)
    to_partner(partner).wait_recv()
    for k in (1, ring - 1, 2, ring - 2, 3, ring - 3, 4):
        fwd_to(k, partner).start()
    take_prefix(partner)
    for k in (1, ring - 1, 2, ring - 2, 3, ring - 3, 4):
        slot = along(ring - k)
        own_to(k, slot).wait_recv()
        take_prefix(slot)

    for o in range(1, n_prompt):
        kv_to(o, flipped(p, flips, o)).wait_recv()
    for a0 in range(0, own_keys, 128):
        got = rkv[a0 // rows_peer : (a0 + 128) // rows_peer].reshape(128, 2 * HEAD)
        at = prefix_keys + a0
        kt[:, at : at + 128] = got[:, :HEAD].T
        va[at : at + 128, :HEAD] = got[:, HEAD:]

    for k in (1, ring - 1, 2, ring - 2, 3, ring - 3, 4):
        slot = along(ring - k) + 1 - 2 * side
        fwd_to(k, slot).wait_recv()
        take_prefix(slot)

    position = c * block + lax.rem(lax.broadcasted_iota(jnp.int32, (2 * block, KEY_TILE), 0), block)
    lane = lax.broadcasted_iota(jnp.int32, (2 * block, KEY_TILE), 1)
    for h in range(0, heads, 2):
        queries = jnp.concatenate([pq[:, h * HEAD : (h + 1) * HEAD], pq[:, (h + 1) * HEAD : (h + 2) * HEAD]], axis=0)
        out = attend_rows(
            queries, kt, va, s_ref, h * block, prefix_keys,
            lambda k0, s: jnp.where(lane + k0 <= position, s, MASKED),
        )
        pout_ref[:, h * HEAD : (h + 1) * HEAD] = out[:block]
        pout_ref[:, (h + 1) * HEAD : (h + 2) * HEAD] = out[block:]

    quad = lax.div(p, 4)
    chunk_rows = 4 * rows_peer

    def chunk(i, carry):
        base = 0
        for b in range(peers - 2):
            base = base + lax.rem(lax.div(quad, 1 << b) + lax.div(i, 1 << b), 2) * (1 << b)
        source = base * 4
        for k in range(4):
            @pl.when(i * 4 + k > 0)
            def _():
                from_peer = base * 4 + flipped(lax.rem(p, 4), flips[:2], k)
                pltpu.make_async_remote_copy(
                    rollout_ref.at[0, 0, from_peer, :, pl.ds(0, span)], rq.at[from_peer],
                    q_send.at[i * 4 + k], q_recv.at[i * 4 + k], device_id=(from_peer, c), device_id_type=MESH,
                ).wait_recv()
        row0 = pl.multiple_of(base * chunk_rows, chunk_rows)
        mine = gcol[pl.ds(row0, chunk_rows), :]
        first = jnp.where(mine >= own_keys // 2, float(own_keys // 2), 0.0)
        for k0 in range(0, own_keys, 128):
            other = grow[0:1, k0 : k0 + 128]
            seen = (other <= mine) & (other >= first)
            bias_ref[:, k0 : k0 + 128] = jnp.where(seen, 0.0, MASKED)

        def masked(k0, s):
            if k0 < prefix_keys:
                return s
            bias = bias_ref[:, k0 - prefix_keys : k0 - prefix_keys + KEY_TILE]
            return s + jnp.concatenate([bias, bias], axis=0)

        rows = rq[pl.ds(source, 4)].reshape(chunk_rows, span)
        for h in range(0, heads, 2):
            queries = jnp.concatenate([rows[:, h * HEAD : (h + 1) * HEAD], rows[:, (h + 1) * HEAD : (h + 2) * HEAD]], axis=0)
            out = attend_rows(queries, kt, va, s_ref, h * chunk_rows, prefix_keys + own_keys, masked)
            rout_ref[pl.ds(row0, chunk_rows), h * HEAD : (h + 1) * HEAD] = out[:chunk_rows]
            rout_ref[pl.ds(row0, chunk_rows), (h + 1) * HEAD : (h + 2) * HEAD] = out[chunk_rows:]
        return carry

    lax.fori_loop(0, n_prompt // 4, chunk, 0)

    to_partner(c).wait_send()
    for k in range(1, ring):
        own_to(k, c).wait_send()
        fwd_to(k, partner).wait_send()
    for o in range(1, n_prompt):
        kv_to(o, p).wait_send()
        q_to(o, p).wait_send()


def place_rows(len_ref, order_ref, tmp_ref, ptmp_ref, rout_ref, pout_ref):
    step = pl.program_id(0)
    rows = rout_ref.shape[0]
    total = tmp_ref.shape[0]
    per_resp = total // len_ref.shape[1] // rows

    @pl.when(step == 0)
    def _():
        pout_ref[...] = ptmp_ref[...]

    limit = len_ref[0, lax.div(step, per_resp)] - lax.rem(step, per_resp) * rows
    order = jnp.broadcast_to(order_ref[...], (128, rows)).T
    live = lax.broadcasted_iota(jnp.int32, (rows, 128), 0) < limit
    order = jnp.where(live, order, -1)
    lane = lax.broadcasted_iota(jnp.int32, (rows, 128), 1)
    pick = jnp.concatenate(
        [jnp.where(order == lane + a0, 1.0, 0.0).astype(jnp.bfloat16) for a0 in range(0, total, 128)], axis=1
    )
    rout_ref[...] = jnp.dot(pick, tmp_ref[...], preferred_element_type=jnp.float32).astype(jnp.bfloat16)


def solution(mesh):
    n_prompt, n_ctx = mesh.shape["prompt"], mesh.shape["ctx"]

    def body(prefix_qkv, rollout, arrival_order, resp_len):
        block, width = prefix_qkv.shape[1:]
        rows_peer = rollout.shape[3]
        span = width - 2 * HEAD
        heads = span // HEAD
        own = n_prompt * rows_peer
        keys = n_ctx * block + own
        order = arrival_order.reshape(1, own)
        dma = pltpu.SemaphoreType.DMA
        any_spec = pl.BlockSpec(memory_space=pl.ANY)
        vmem_spec = pl.BlockSpec(memory_space=pltpu.VMEM)
        ptmp, tmp = pl.pallas_call(
            functools.partial(gather_attend, n_prompt, n_ctx, heads),
            out_shape=(
                jax.ShapeDtypeStruct((block, span), jnp.bfloat16),
                jax.ShapeDtypeStruct((own, span), jnp.bfloat16),
            ),
            in_specs=[any_spec, any_spec, vmem_spec],
            out_specs=(vmem_spec, vmem_spec),
            scratch_shapes=[
                pltpu.VMEM((n_ctx, block, 2 * HEAD), jnp.bfloat16),
                pltpu.VMEM((n_prompt, rows_peer, 2 * HEAD), jnp.bfloat16),
                pltpu.VMEM((n_prompt, rows_peer, span), jnp.bfloat16),
                pltpu.VMEM((block, span), jnp.bfloat16),
                pltpu.VMEM((HEAD, keys), jnp.bfloat16),
                pltpu.VMEM((keys, 2 * HEAD), jnp.bfloat16),
                pltpu.VMEM((4 * 128, keys), jnp.float32),
                pltpu.VMEM((4 * rows_peer, own), jnp.float32),
                pltpu.VMEM((own, 128), jnp.float32),
                pltpu.VMEM((8, own), jnp.float32),
                dma((4,)),
                dma((1,)),
                dma((1,)),
                dma((n_ctx // 2,)),
                dma((n_ctx // 2,)),
                dma((n_ctx // 2,)),
                dma((n_ctx // 2,)),
                dma((n_prompt,)),
                dma((n_prompt,)),
                dma((n_prompt,)),
                dma((n_prompt,)),
            ],
            compiler_params=pltpu.CompilerParams(collective_id=0, has_side_effects=True),
            name="gather_attend",
        )(prefix_qkv, rollout, order)
        step_rows = 256
        out, pout = pl.pallas_call(
            place_rows,
            grid=(own // step_rows,),
            out_shape=(
                jax.ShapeDtypeStruct((own, span), jnp.bfloat16),
                jax.ShapeDtypeStruct((block, span), jnp.bfloat16),
            ),
            in_specs=[
                pl.BlockSpec(memory_space=pltpu.SMEM),
                pl.BlockSpec((1, step_rows), lambda i: (0, i)),
                pl.BlockSpec((own, span), lambda i: (0, 0)),
                pl.BlockSpec((block, span), lambda i: (0, 0)),
            ],
            out_specs=(
                pl.BlockSpec((step_rows, span), lambda i: (i, 0)),
                pl.BlockSpec((block, span), lambda i: (0, 0)),
            ),
            name="place_rows",
        )(resp_len, order, tmp, ptmp)
        per = resp_len.shape[1]
        return pout[None], out.reshape(1, per, own // per, span)

    spec = P("prompt", "ctx", None)
    return jax.shard_map(
        body,
        mesh=mesh,
        in_specs=(spec, P("prompt", "ctx", None, None, None), spec, P("prompt", "ctx")),
        out_specs=(spec, P("prompt", "ctx", None, None)),
        check_vma=False,
    )
```

```python
import functools
import math

import jax
import jax.numpy as jnp
from jax import lax
from jax.experimental import pallas as pl
from jax.experimental.pallas import tpu as pltpu
from jax.sharding import PartitionSpec as P

HEAD = 128
MASKED = -1e30
MESH = pl.DeviceIdType.MESH
SCALE2 = HEAD ** (-0.5) * math.log2(math.e)
KEY_TILE = 512
UNIT = 2
NEAR = (1, 7, 2, 6)


def bit_flips(index, bits):
    return [(1 - 2 * lax.rem(lax.div(index, 1 << b), 2)) * (1 << b) for b in range(bits)]


def flipped(index, flips, mask):
    for b, step in enumerate(flips):
        if mask >> b & 1:
            index = index + step
    return index


def score_tile(queries, kt, s_ref, k0, top, extra):
    s = jnp.dot(queries, kt[:, k0 : k0 + KEY_TILE], preferred_element_type=jnp.float32)
    s = extra(k0, s)
    s_ref[:, k0 : k0 + KEY_TILE] = s
    for l0 in range(0, KEY_TILE, 128):
        part = s[:, l0 : l0 + 128]
        top = part if top is None else jnp.maximum(top, part)
    return top


def weigh_tile(va, s_ref, k0, top, carried):
    weights = jnp.exp2((s_ref[:, k0 : k0 + KEY_TILE] - top) * SCALE2)
    row_sum, total = carried
    for l0 in range(0, KEY_TILE, 128):
        part = weights[:, l0 : l0 + 128]
        row_sum = part if row_sum is None else row_sum + part
    part = jnp.dot(weights.astype(jnp.bfloat16), va[k0 : k0 + KEY_TILE, :], preferred_element_type=jnp.float32)
    return row_sum, part if total is None else total + part


def finish_rows(carried):
    row_sum, total = carried
    return (total / jnp.sum(row_sum, axis=-1, keepdims=True)).astype(jnp.bfloat16)


def stack_heads(rows, h):
    return jnp.concatenate([rows[:, g * HEAD : (g + 1) * HEAD] for g in range(h, h + UNIT)], axis=0)


def gather_attend(
    n_prompt, n_ctx, heads,
    prefix_ref, rollout_ref, order_ref, pout_ref, rout_ref,
    pkv, rkv, rq, pq, kt, va, s_ref, top_ref, bias_ref, gcol, grow,
    local_sem, part_send, part_recv, own_send, own_recv, fwd_send, fwd_recv, own_hop_send, own_hop_recv, fwd_hop_send, fwd_hop_recv,
    kv_send, kv_recv, q_send, q_recv,
):
    p = lax.axis_index("prompt")
    c = lax.axis_index("ctx")
    span = heads * HEAD
    width = span + 2 * HEAD
    peers = n_prompt.bit_length() - 1
    flips = bit_flips(p, peers)
    ring = n_ctx // 2
    z, side = lax.div(c, 2), lax.rem(c, 2)
    partner = c + 1 - 2 * side
    rows_peer = rkv.shape[1]
    block = pkv.shape[1]
    prefix_keys = n_ctx * block
    own_keys = n_prompt * rows_peer

    def along(step):
        return lax.rem(z + step, ring) * 2 + side

    barrier = pltpu.get_barrier_semaphore()
    for o in range(1, n_prompt):
        pl.semaphore_signal(barrier, inc=1, device_id=(flipped(p, flips, o), c), device_id_type=MESH)
    pl.semaphore_signal(barrier, inc=1, device_id=(p, partner), device_id_type=MESH)
    for k in NEAR:
        pl.semaphore_signal(barrier, inc=1, device_id=(p, along(k)), device_id_type=MESH)

    own_block = prefix_ref.at[0, :, pl.ds(span, 2 * HEAD)]
    local = [
        pltpu.make_async_copy(own_block, pkv.at[c], local_sem.at[0]),
        pltpu.make_async_copy(prefix_ref.at[0, :, pl.ds(0, span)], pq, local_sem.at[1]),
        pltpu.make_async_copy(rollout_ref.at[0, 0, p, :, pl.ds(span, 2 * HEAD)], rkv.at[p], local_sem.at[2]),
        pltpu.make_async_copy(rollout_ref.at[0, 0, p, :, pl.ds(0, span)], rq.at[p], local_sem.at[3]),
    ]
    for copy in local:
        copy.start()

    def to_partner(slot):
        return pltpu.make_async_remote_copy(
            own_block, pkv.at[slot], part_send.at[0], part_recv.at[0], device_id=(p, partner), device_id_type=MESH
        )

    def own_to(k, slot):
        return pltpu.make_async_remote_copy(
            own_block, pkv.at[slot], own_send.at[k], own_recv.at[k], device_id=(p, along(k)), device_id_type=MESH
        )

    def fwd_to(k, slot):
        return pltpu.make_async_remote_copy(
            pkv.at[partner], pkv.at[slot], fwd_send.at[k], fwd_recv.at[k], device_id=(p, along(k)), device_id_type=MESH
        )

    def hop_copies(own, arrived):
        slot = along if own else (lambda k: along(k) + 1 - 2 * side)
        send, recv = (own_hop_send, own_hop_recv) if own else (fwd_hop_send, fwd_hop_recv)
        half = block // 2
        low, high = pl.ds(0, half), pl.ds(half, half)
        before, after = pkv.at[slot(ring - 2)], pkv.at[slot(2)]
        ends = [before, before.at[low], after, after.at[high]]
        if arrived:
            ends = [pkv.at[slot(ring - 3)], pkv.at[slot(4), low], pkv.at[slot(3)], pkv.at[slot(4), high]]
        starts = [before, before.at[low], after, after.at[high]]
        return [
            pltpu.make_async_remote_copy(
                start, end, send.at[j], recv.at[j], device_id=(p, along(k)), device_id_type=MESH
            )
            for j, (start, end, k) in enumerate(zip(starts, ends, (1, 2, ring - 1, ring - 2)))
        ]

    def kv_to(o, slot):
        there = flipped(p, flips, o)
        return pltpu.make_async_remote_copy(
            rollout_ref.at[0, 0, there, :, pl.ds(span, 2 * HEAD)], rkv.at[slot],
            kv_send.at[o], kv_recv.at[o], device_id=(there, c), device_id_type=MESH,
        )

    def q_to(o, slot):
        there = flipped(p, flips, o)
        return pltpu.make_async_remote_copy(
            rollout_ref.at[0, 0, there, :, pl.ds(0, span)], rq.at[slot],
            q_send.at[o], q_recv.at[o], device_id=(there, c), device_id_type=MESH,
        )

    order = order_ref[...]
    place = lax.broadcasted_iota(jnp.int32, (128, own_keys), 1).astype(jnp.float32)
    for a0 in range(0, own_keys, 128):
        arrived = lax.broadcasted_iota(jnp.int32, (128, own_keys), 0) + a0
        at = jnp.sum(jnp.where(order == arrived, place, 0.0), axis=-1, keepdims=True)
        at = jnp.broadcast_to(at, (128, 128))
        gcol[a0 : a0 + 128, :] = at
        grow[:, a0 : a0 + 128] = at.T[:8]

    pl.semaphore_wait(barrier, n_prompt + len(NEAR))
    half = n_prompt // 2
    to_partner(c).start()
    for k in NEAR:
        own_to(k, c).start()
    for o in list(range(half, n_prompt)) + list(range(half // 2, half)) + list(range(1, half // 2)):
        kv_to(o, p).start()
    for o in range(1, n_prompt):
        q_to(o, p).start()

    for copy in local:
        copy.wait()

    def take_prefix(slot):
        rows = pl.ds(pl.multiple_of(slot * block, block), block)
        got = pkv[slot]
        kt[:, rows] = got[:, :HEAD].T
        va[rows, :] = got[:, HEAD:]

    def other(k):
        return along(k) + 1 - 2 * side

    take_prefix(c)
    to_partner(partner).wait_recv()
    for k in NEAR:
        fwd_to(k, partner).start()
    own_hops = hop_copies(True, False)
    own_to(2, along(ring - 2)).wait_recv()
    own_hops[0].start()
    own_hops[1].start()
    own_to(ring - 2, along(2)).wait_recv()
    own_hops[2].start()
    own_hops[3].start()
    take_prefix(partner)
    take_prefix(along(2))
    take_prefix(along(ring - 2))
    for k in (1, ring - 1):
        own_to(k, along(ring - k)).wait_recv()
        take_prefix(along(ring - k))
    fwd_hops = hop_copies(False, False)
    fwd_to(2, other(ring - 2)).wait_recv()
    fwd_hops[0].start()
    fwd_hops[1].start()
    fwd_to(ring - 2, other(2)).wait_recv()
    fwd_hops[2].start()
    fwd_hops[3].start()
    take_prefix(other(2))
    take_prefix(other(ring - 2))
    for k in (1, ring - 1):
        fwd_to(k, other(ring - k)).wait_recv()
        take_prefix(other(ring - k))
    for o in range(1, n_prompt):
        kv_to(o, flipped(p, flips, o)).wait_recv()
    for a0 in range(0, own_keys, 128):
        got = rkv[a0 // rows_peer : (a0 + 128) // rows_peer].reshape(128, 2 * HEAD)
        at = prefix_keys + a0
        kt[:, at : at + 128] = got[:, :HEAD].T
        va[at : at + 128, :] = got[:, HEAD:]
    for own in (True, False):
        for copy in hop_copies(own, True):
            copy.wait_recv()
        for k in (3, 4, 5):
            take_prefix(along(k) if own else other(k))

    position = c * block + lax.rem(lax.broadcasted_iota(jnp.int32, (UNIT * block, KEY_TILE), 0), block)
    lane = lax.broadcasted_iota(jnp.int32, (UNIT * block, KEY_TILE), 1)

    def causal(k0, s):
        return jnp.where(lane + k0 <= position, s, MASKED)

    for h in range(0, heads, UNIT):
        queries = stack_heads(pq, h)
        top = None
        for k0 in range(0, prefix_keys, KEY_TILE):
            top = score_tile(queries, kt, s_ref.at[0], k0, top, causal)
        top = jnp.max(top, axis=-1, keepdims=True)
        carried = None, None
        for k0 in range(0, prefix_keys, KEY_TILE):
            carried = weigh_tile(va, s_ref.at[0], k0, top, carried)
        out = finish_rows(carried)
        for g in range(UNIT):
            pout_ref[:, (h + g) * HEAD : (h + g + 1) * HEAD] = out[g * block : (g + 1) * block]

    quad = lax.div(p, 4)
    chunk_rows = 4 * rows_peer
    chunks = n_prompt // 4
    keys = prefix_keys + own_keys

    def base_of(i):
        base = 0
        for b in range(peers - 2):
            base = base + lax.rem(lax.div(quad, 1 << b) + lax.div(i, 1 << b), 2) * (1 << b)
        return base

    def get_chunk(i):
        base = base_of(i)
        for k in range(4):
            @pl.when(i * 4 + k > 0)
            def _():
                from_peer = base * 4 + flipped(lax.rem(p, 4), flips[:2], k)
                pltpu.make_async_remote_copy(
                    rollout_ref.at[0, 0, from_peer, :, pl.ds(0, span)], rq.at[from_peer],
                    q_send.at[i * 4 + k], q_recv.at[i * 4 + k], device_id=(from_peer, c), device_id_type=MESH,
                ).wait_recv()
        mine = gcol[pl.ds(pl.multiple_of(base * chunk_rows, chunk_rows), chunk_rows), :]
        first = jnp.where(mine >= own_keys // 2, float(own_keys // 2), 0.0)
        for k0 in range(0, own_keys, 128):
            other = grow[0:1, k0 : k0 + 128]
            seen = (other <= mine) & (other >= first)
            bias_ref[:, k0 : k0 + 128] = jnp.where(seen, 0.0, MASKED)

    def masked(k0, s):
        if k0 < prefix_keys:
            return s
        bias = bias_ref[:, k0 - prefix_keys : k0 - prefix_keys + KEY_TILE]
        return s + jnp.concatenate([bias] * UNIT, axis=0)

    def queries_of(i, h):
        return stack_heads(rq[pl.ds(base_of(i) * 4, 4)].reshape(chunk_rows, span), h)

    get_chunk(0)
    queries = queries_of(0, 0)
    top = None
    for k0 in range(0, keys, KEY_TILE):
        top = score_tile(queries, kt, s_ref.at[0], k0, top, masked)
    top_ref[...] = jnp.broadcast_to(jnp.max(top, axis=-1, keepdims=True), top.shape)

    def chunk(i, last):
        row0 = pl.multiple_of(base_of(i) * chunk_rows, chunk_rows)
        units = heads // UNIT
        for u in range(units):
            ahead = not (last and u == units - 1)
            if not ahead:
                pass
            elif u == units - 1:
                get_chunk(i + 1)
                queries = queries_of(i + 1, 0)
            else:
                queries = queries_of(i, (u + 1) * UNIT)
            now_top = top_ref[:, 0:1]
            top, carried = None, (None, None)
            for k0 in range(0, keys, KEY_TILE):
                if ahead:
                    top = score_tile(queries, kt, s_ref.at[(u + 1) % 2], k0, top, masked)
                carried = weigh_tile(va, s_ref.at[u % 2], k0, now_top, carried)
            if ahead:
                top_ref[...] = jnp.broadcast_to(jnp.max(top, axis=-1, keepdims=True), top.shape)
            out = finish_rows(carried)
            for g in range(UNIT):
                h = u * UNIT + g
                rout_ref[pl.ds(row0, chunk_rows), h * HEAD : (h + 1) * HEAD] = out[g * chunk_rows : (g + 1) * chunk_rows]

    @pl.loop(0, chunks - 1)
    def _(i):
        chunk(i, False)

    chunk(chunks - 1, True)

    to_partner(c).wait_send()
    for k in NEAR:
        own_to(k, c).wait_send()
        fwd_to(k, partner).wait_send()
    for copy in own_hops + fwd_hops:
        copy.wait_send()
    for o in range(1, n_prompt):
        kv_to(o, p).wait_send()
        q_to(o, p).wait_send()


def place_rows(len_ref, order_ref, tmp_ref, ptmp_ref, rout_ref, pout_ref):
    step = pl.program_id(0)
    rows = rout_ref.shape[0]
    total = tmp_ref.shape[0]
    per_resp = total // len_ref.shape[1] // rows

    @pl.when(step == 0)
    def _():
        pout_ref[...] = ptmp_ref[...]

    limit = len_ref[0, lax.div(step, per_resp)] - lax.rem(step, per_resp) * rows
    order = jnp.broadcast_to(order_ref[...], (128, rows)).T
    live = lax.broadcasted_iota(jnp.int32, (rows, 128), 0) < limit
    order = jnp.where(live, order, -1)
    lane = lax.broadcasted_iota(jnp.int32, (rows, 128), 1)
    pick = jnp.concatenate(
        [jnp.where(order == lane + a0, 1.0, 0.0).astype(jnp.bfloat16) for a0 in range(0, total, 128)], axis=1
    )
    rout_ref[...] = jnp.dot(pick, tmp_ref[...], preferred_element_type=jnp.float32).astype(jnp.bfloat16)


def solution(mesh):
    n_prompt, n_ctx = mesh.shape["prompt"], mesh.shape["ctx"]

    def body(prefix_qkv, rollout, arrival_order, resp_len):
        block, width = prefix_qkv.shape[1:]
        rows_peer = rollout.shape[3]
        span = width - 2 * HEAD
        heads = span // HEAD
        own = n_prompt * rows_peer
        keys = n_ctx * block + own
        order = arrival_order.reshape(1, own)
        dma = pltpu.SemaphoreType.DMA
        any_spec = pl.BlockSpec(memory_space=pl.ANY)
        vmem_spec = pl.BlockSpec(memory_space=pltpu.VMEM)
        ptmp, tmp = pl.pallas_call(
            functools.partial(gather_attend, n_prompt, n_ctx, heads),
            out_shape=(
                jax.ShapeDtypeStruct((block, span), jnp.bfloat16),
                jax.ShapeDtypeStruct((own, span), jnp.bfloat16),
            ),
            in_specs=[any_spec, any_spec, vmem_spec],
            out_specs=(vmem_spec, vmem_spec),
            scratch_shapes=[
                pltpu.VMEM((n_ctx, block, 2 * HEAD), jnp.bfloat16),
                pltpu.VMEM((n_prompt, rows_peer, 2 * HEAD), jnp.bfloat16),
                pltpu.VMEM((n_prompt, rows_peer, span), jnp.bfloat16),
                pltpu.VMEM((block, span), jnp.bfloat16),
                pltpu.VMEM((HEAD, keys), jnp.bfloat16),
                pltpu.VMEM((keys, HEAD), jnp.bfloat16),
                pltpu.VMEM((2, UNIT * 128, keys), jnp.float32),
                pltpu.VMEM((UNIT * 128, 128), jnp.float32),
                pltpu.VMEM((4 * rows_peer, own), jnp.float32),
                pltpu.VMEM((own, 128), jnp.float32),
                pltpu.VMEM((8, own), jnp.float32),
                dma((4,)),
                dma((1,)),
                dma((1,)),
                dma((n_ctx // 2,)),
                dma((n_ctx // 2,)),
                dma((n_ctx // 2,)),
                dma((n_ctx // 2,)),
                dma((4,)),
                dma((4,)),
                dma((4,)),
                dma((4,)),
                dma((n_prompt,)),
                dma((n_prompt,)),
                dma((n_prompt,)),
                dma((n_prompt,)),
            ],
            compiler_params=pltpu.CompilerParams(collective_id=0, has_side_effects=True),
            name="gather_attend",
        )(prefix_qkv, rollout, order)
        step_rows = 256
        out, pout = pl.pallas_call(
            place_rows,
            grid=(own // step_rows,),
            out_shape=(
                jax.ShapeDtypeStruct((own, span), jnp.bfloat16),
                jax.ShapeDtypeStruct((block, span), jnp.bfloat16),
            ),
            in_specs=[
                pl.BlockSpec(memory_space=pltpu.SMEM),
                pl.BlockSpec((1, step_rows), lambda i: (0, i)),
                pl.BlockSpec((own, span), lambda i: (0, 0)),
                pl.BlockSpec((block, span), lambda i: (0, 0)),
            ],
            out_specs=(
                pl.BlockSpec((step_rows, span), lambda i: (i, 0)),
                pl.BlockSpec((block, span), lambda i: (0, 0)),
            ),
            name="place_rows",
        )(resp_len, order, tmp, ptmp)
        per = resp_len.shape[1]
        return pout[None], out.reshape(1, per, own // per, span)

    spec = P("prompt", "ctx", None)
    return jax.shard_map(
        body,
        mesh=mesh,
        in_specs=(spec, P("prompt", "ctx", None, None, None), spec, P("prompt", "ctx")),
        out_specs=(spec, P("prompt", "ctx", None, None)),
        check_vma=False,
    )
```

```python
import functools
import math

import jax
import jax.numpy as jnp
from jax import lax
from jax.experimental import pallas as pl
from jax.experimental.pallas import tpu as pltpu
from jax.sharding import PartitionSpec as P

HEAD = 128
MASKED = -1e30
MESH = pl.DeviceIdType.MESH
SCALE2 = HEAD ** (-0.5) * math.log2(math.e)
KEY_TILE = 512
UNIT = 2
NEAR = (1, 7, 2, 6)


def bit_flips(index, bits):
    return [(1 - 2 * lax.rem(lax.div(index, 1 << b), 2)) * (1 << b) for b in range(bits)]


def flipped(index, flips, mask):
    for b, step in enumerate(flips):
        if mask >> b & 1:
            index = index + step
    return index


def score_tile(queries, kt, s_ref, k0, top, extra):
    s = jnp.dot(queries, kt[:, k0 : k0 + KEY_TILE], preferred_element_type=jnp.float32)
    s = extra(k0, s)
    s_ref[:, k0 : k0 + KEY_TILE] = s
    for l0 in range(0, KEY_TILE, 128):
        part = s[:, l0 : l0 + 128]
        top = part if top is None else jnp.maximum(top, part)
    return top


def weigh_tile(va, s_ref, k0, top, carried):
    weights = jnp.exp2((s_ref[:, k0 : k0 + KEY_TILE] - top) * SCALE2)
    row_sum, total = carried
    for l0 in range(0, KEY_TILE, 128):
        part = weights[:, l0 : l0 + 128]
        row_sum = part if row_sum is None else row_sum + part
    part = jnp.dot(weights.astype(jnp.bfloat16), va[k0 : k0 + KEY_TILE, :], preferred_element_type=jnp.float32)
    return row_sum, part if total is None else total + part


def finish_rows(carried):
    row_sum, total = carried
    return (total / jnp.sum(row_sum, axis=-1, keepdims=True)).astype(jnp.bfloat16)


def stack_heads(rows, h):
    return jnp.concatenate([rows[:, g * HEAD : (g + 1) * HEAD] for g in range(h, h + UNIT)], axis=0)


def gather_attend(
    n_prompt, n_ctx, heads,
    prefix_ref, rollout_ref, order_ref, pout_ref, rout_ref,
    pkv, rkv, rq, pq, pres, rres, out_sem, kt, va, s_ref, top_ref, bias_ref, gcol, grow,
    local_sem, part_send, part_recv, own_send, own_recv, fwd_send, fwd_recv, own_hop_send, own_hop_recv, fwd_hop_send, fwd_hop_recv,
    kv_send, kv_recv, q_send, q_recv,
):
    p = lax.axis_index("prompt")
    c = lax.axis_index("ctx")
    span = heads * HEAD
    width = span + 2 * HEAD
    peers = n_prompt.bit_length() - 1
    flips = bit_flips(p, peers)
    ring = n_ctx // 2
    z, side = lax.div(c, 2), lax.rem(c, 2)
    partner = c + 1 - 2 * side
    rows_peer = rkv.shape[1]
    block = pkv.shape[1]
    prefix_keys = n_ctx * block
    own_keys = n_prompt * rows_peer

    def along(step):
        return lax.rem(z + step, ring) * 2 + side

    barrier = pltpu.get_barrier_semaphore()
    for o in range(1, n_prompt):
        pl.semaphore_signal(barrier, inc=1, device_id=(flipped(p, flips, o), c), device_id_type=MESH)
    pl.semaphore_signal(barrier, inc=1, device_id=(p, partner), device_id_type=MESH)
    for k in NEAR:
        pl.semaphore_signal(barrier, inc=1, device_id=(p, along(k)), device_id_type=MESH)

    own_block = prefix_ref.at[0, :, pl.ds(span, 2 * HEAD)]
    local = [
        pltpu.make_async_copy(own_block, pkv.at[c], local_sem.at[0]),
        pltpu.make_async_copy(prefix_ref.at[0, :, pl.ds(0, span)], pq, local_sem.at[1]),
        pltpu.make_async_copy(rollout_ref.at[0, 0, p, :, pl.ds(span, 2 * HEAD)], rkv.at[p], local_sem.at[2]),
        pltpu.make_async_copy(rollout_ref.at[0, 0, p, :, pl.ds(0, span)], rq.at[p], local_sem.at[3]),
    ]
    for copy in local:
        copy.start()

    def to_partner(slot):
        return pltpu.make_async_remote_copy(
            own_block, pkv.at[slot], part_send.at[0], part_recv.at[0], device_id=(p, partner), device_id_type=MESH
        )

    def own_to(k, slot):
        return pltpu.make_async_remote_copy(
            own_block, pkv.at[slot], own_send.at[k], own_recv.at[k], device_id=(p, along(k)), device_id_type=MESH
        )

    def fwd_to(k, slot):
        return pltpu.make_async_remote_copy(
            pkv.at[partner], pkv.at[slot], fwd_send.at[k], fwd_recv.at[k], device_id=(p, along(k)), device_id_type=MESH
        )

    def hop_copies(own, arrived):
        slot = along if own else (lambda k: along(k) + 1 - 2 * side)
        send, recv = (own_hop_send, own_hop_recv) if own else (fwd_hop_send, fwd_hop_recv)
        half = block // 2
        low, high = pl.ds(0, half), pl.ds(half, half)
        before, after = pkv.at[slot(ring - 2)], pkv.at[slot(2)]
        ends = [before, before.at[low], after, after.at[high]]
        if arrived:
            ends = [pkv.at[slot(ring - 3)], pkv.at[slot(4), low], pkv.at[slot(3)], pkv.at[slot(4), high]]
        starts = [before, before.at[low], after, after.at[high]]
        return [
            pltpu.make_async_remote_copy(
                start, end, send.at[j], recv.at[j], device_id=(p, along(k)), device_id_type=MESH
            )
            for j, (start, end, k) in enumerate(zip(starts, ends, (1, 2, ring - 1, ring - 2)))
        ]

    def kv_to(o, slot):
        there = flipped(p, flips, o)
        return pltpu.make_async_remote_copy(
            rollout_ref.at[0, 0, there, :, pl.ds(span, 2 * HEAD)], rkv.at[slot],
            kv_send.at[o], kv_recv.at[o], device_id=(there, c), device_id_type=MESH,
        )

    def q_to(o, slot):
        there = flipped(p, flips, o)
        return pltpu.make_async_remote_copy(
            rollout_ref.at[0, 0, there, :, pl.ds(0, span)], rq.at[slot],
            q_send.at[o], q_recv.at[o], device_id=(there, c), device_id_type=MESH,
        )

    order = order_ref[...]
    place = lax.broadcasted_iota(jnp.int32, (128, own_keys), 1).astype(jnp.float32)
    for a0 in range(0, own_keys, 128):
        arrived = lax.broadcasted_iota(jnp.int32, (128, own_keys), 0) + a0
        at = jnp.sum(jnp.where(order == arrived, place, 0.0), axis=-1, keepdims=True)
        at = jnp.broadcast_to(at, (128, 128))
        gcol[a0 : a0 + 128, :] = at
        grow[:, a0 : a0 + 128] = at.T[:8]

    pl.semaphore_wait(barrier, n_prompt + len(NEAR))
    half = n_prompt // 2
    to_partner(c).start()
    for k in NEAR:
        own_to(k, c).start()
    for o in list(range(half, n_prompt)) + list(range(half // 2, half)) + list(range(1, half // 2)):
        kv_to(o, p).start()
    for o in range(1, n_prompt):
        q_to(o, p).start()

    for copy in local:
        copy.wait()

    def take_prefix(slot):
        rows = pl.ds(pl.multiple_of(slot * block, block), block)
        got = pkv[slot]
        kt[:, rows] = got[:, :HEAD].T
        va[rows, :] = got[:, HEAD:]

    def other(k):
        return along(k) + 1 - 2 * side

    take_prefix(c)
    to_partner(partner).wait_recv()
    for k in NEAR:
        fwd_to(k, partner).start()
    own_hops = hop_copies(True, False)
    own_to(2, along(ring - 2)).wait_recv()
    own_hops[0].start()
    own_hops[1].start()
    own_to(ring - 2, along(2)).wait_recv()
    own_hops[2].start()
    own_hops[3].start()
    take_prefix(partner)
    take_prefix(along(2))
    take_prefix(along(ring - 2))
    for k in (1, ring - 1):
        own_to(k, along(ring - k)).wait_recv()
        take_prefix(along(ring - k))
    fwd_hops = hop_copies(False, False)
    fwd_to(2, other(ring - 2)).wait_recv()
    fwd_hops[0].start()
    fwd_hops[1].start()
    fwd_to(ring - 2, other(2)).wait_recv()
    fwd_hops[2].start()
    fwd_hops[3].start()
    take_prefix(other(2))
    take_prefix(other(ring - 2))
    for k in (1, ring - 1):
        fwd_to(k, other(ring - k)).wait_recv()
        take_prefix(other(ring - k))
    for o in range(1, n_prompt):
        kv_to(o, flipped(p, flips, o)).wait_recv()
    for a0 in range(0, own_keys, 128):
        got = rkv[a0 // rows_peer : (a0 + 128) // rows_peer].reshape(128, 2 * HEAD)
        at = prefix_keys + a0
        kt[:, at : at + 128] = got[:, :HEAD].T
        va[at : at + 128, :] = got[:, HEAD:]
    for own in (True, False):
        for copy in hop_copies(own, True):
            copy.wait_recv()
        for k in (3, 4, 5):
            take_prefix(along(k) if own else other(k))

    position = c * block + lax.rem(lax.broadcasted_iota(jnp.int32, (UNIT * block, KEY_TILE), 0), block)
    lane = lax.broadcasted_iota(jnp.int32, (UNIT * block, KEY_TILE), 1)

    def causal(k0, s):
        return jnp.where(lane + k0 <= position, s, MASKED)

    for h in range(0, heads, UNIT):
        queries = stack_heads(pq, h)
        top = None
        for k0 in range(0, prefix_keys, KEY_TILE):
            top = score_tile(queries, kt, s_ref.at[0], k0, top, causal)
        top = jnp.max(top, axis=-1, keepdims=True)
        carried = None, None
        for k0 in range(0, prefix_keys, KEY_TILE):
            carried = weigh_tile(va, s_ref.at[0], k0, top, carried)
        out = finish_rows(carried)
        for g in range(UNIT):
            pres[:, (h + g) * HEAD : (h + g + 1) * HEAD] = out[g * block : (g + 1) * block]

    pout = pltpu.make_async_copy(pres, pout_ref, local_sem.at[0])
    pout.start()

    quad = lax.div(p, 4)
    chunk_rows = 4 * rows_peer
    chunks = n_prompt // 4
    keys = prefix_keys + own_keys

    def base_of(i):
        base = 0
        for b in range(peers - 2):
            base = base + lax.rem(lax.div(quad, 1 << b) + lax.div(i, 1 << b), 2) * (1 << b)
        return base

    def get_chunk(i):
        base = base_of(i)
        for k in range(4):
            @pl.when(i * 4 + k > 0)
            def _():
                from_peer = base * 4 + flipped(lax.rem(p, 4), flips[:2], k)
                pltpu.make_async_remote_copy(
                    rollout_ref.at[0, 0, from_peer, :, pl.ds(0, span)], rq.at[from_peer],
                    q_send.at[i * 4 + k], q_recv.at[i * 4 + k], device_id=(from_peer, c), device_id_type=MESH,
                ).wait_recv()
        mine = gcol[pl.ds(pl.multiple_of(base * chunk_rows, chunk_rows), chunk_rows), :]
        first = jnp.where(mine >= own_keys // 2, float(own_keys // 2), 0.0)
        for k0 in range(0, own_keys, 128):
            other = grow[0:1, k0 : k0 + 128]
            seen = (other <= mine) & (other >= first)
            bias_ref[:, k0 : k0 + 128] = jnp.where(seen, 0.0, MASKED)

    def masked(k0, s):
        if k0 < prefix_keys:
            return s
        bias = bias_ref[:, k0 - prefix_keys : k0 - prefix_keys + KEY_TILE]
        return s + jnp.concatenate([bias] * UNIT, axis=0)

    def queries_of(i, h):
        return stack_heads(rq[pl.ds(base_of(i) * 4, 4)].reshape(chunk_rows, span), h)

    get_chunk(0)
    queries = queries_of(0, 0)
    top = None
    for k0 in range(0, keys, KEY_TILE):
        top = score_tile(queries, kt, s_ref.at[0], k0, top, masked)
    top_ref[...] = jnp.broadcast_to(jnp.max(top, axis=-1, keepdims=True), top.shape)

    def chunk(i, last):
        row0 = pl.multiple_of(base_of(i) * chunk_rows, chunk_rows)
        units = heads // UNIT
        for u in range(units):
            ahead = not (last and u == units - 1)
            if not ahead:
                pass
            elif u == units - 1:
                get_chunk(i + 1)
                queries = queries_of(i + 1, 0)
            else:
                queries = queries_of(i, (u + 1) * UNIT)
            now_top = top_ref[:, 0:1]
            top, carried = None, (None, None)
            for k0 in range(0, keys, KEY_TILE):
                if ahead:
                    top = score_tile(queries, kt, s_ref.at[(u + 1) % 2], k0, top, masked)
                carried = weigh_tile(va, s_ref.at[u % 2], k0, now_top, carried)
            if ahead:
                top_ref[...] = jnp.broadcast_to(jnp.max(top, axis=-1, keepdims=True), top.shape)
            out = finish_rows(carried)
            for g in range(UNIT):
                h = u * UNIT + g
                rres[pl.ds(row0, chunk_rows), h * HEAD : (h + 1) * HEAD] = out[g * chunk_rows : (g + 1) * chunk_rows]
        leave(i).start()

    def leave(i):
        rows = pl.ds(pl.multiple_of(base_of(i) * chunk_rows, chunk_rows), chunk_rows)
        return pltpu.make_async_copy(rres.at[rows], rout_ref.at[rows], out_sem.at[i])

    @pl.loop(0, chunks - 1)
    def _(i):
        chunk(i, False)

    chunk(chunks - 1, True)
    pout.wait()
    for i in range(chunks):
        leave(i).wait()

    to_partner(c).wait_send()
    for k in NEAR:
        own_to(k, c).wait_send()
        fwd_to(k, partner).wait_send()
    for copy in own_hops + fwd_hops:
        copy.wait_send()
    for o in range(1, n_prompt):
        kv_to(o, p).wait_send()
        q_to(o, p).wait_send()


def place_rows(len_ref, order_ref, tmp_ref, ptmp_ref, rout_ref, pout_ref):
    step = pl.program_id(0)
    rows = rout_ref.shape[0]
    total = tmp_ref.shape[0]
    per_resp = total // len_ref.shape[1] // rows

    @pl.when(step == 0)
    def _():
        pout_ref[...] = ptmp_ref[...]

    limit = len_ref[0, lax.div(step, per_resp)] - lax.rem(step, per_resp) * rows
    order = jnp.broadcast_to(order_ref[...], (128, rows)).T
    live = lax.broadcasted_iota(jnp.int32, (rows, 128), 0) < limit
    order = jnp.where(live, order, -1)
    lane = lax.broadcasted_iota(jnp.int32, (rows, 128), 1)
    pick = jnp.concatenate(
        [jnp.where(order == lane + a0, 1.0, 0.0).astype(jnp.bfloat16) for a0 in range(0, total, 128)], axis=1
    )
    rout_ref[...] = jnp.dot(pick, tmp_ref[...], preferred_element_type=jnp.float32).astype(jnp.bfloat16)


def solution(mesh):
    n_prompt, n_ctx = mesh.shape["prompt"], mesh.shape["ctx"]

    def body(prefix_qkv, rollout, arrival_order, resp_len):
        block, width = prefix_qkv.shape[1:]
        rows_peer = rollout.shape[3]
        span = width - 2 * HEAD
        heads = span // HEAD
        own = n_prompt * rows_peer
        keys = n_ctx * block + own
        order = arrival_order.reshape(1, own)
        dma = pltpu.SemaphoreType.DMA
        any_spec = pl.BlockSpec(memory_space=pl.ANY)
        vmem_spec = pl.BlockSpec(memory_space=pltpu.VMEM)
        ptmp, tmp = pl.pallas_call(
            functools.partial(gather_attend, n_prompt, n_ctx, heads),
            out_shape=(
                jax.ShapeDtypeStruct((block, span), jnp.bfloat16),
                jax.ShapeDtypeStruct((own, span), jnp.bfloat16),
            ),
            in_specs=[any_spec, any_spec, vmem_spec],
            out_specs=(any_spec, any_spec),
            scratch_shapes=[
                pltpu.VMEM((n_ctx, block, 2 * HEAD), jnp.bfloat16),
                pltpu.VMEM((n_prompt, rows_peer, 2 * HEAD), jnp.bfloat16),
                pltpu.VMEM((n_prompt, rows_peer, span), jnp.bfloat16),
                pltpu.VMEM((block, span), jnp.bfloat16),
                pltpu.VMEM((block, span), jnp.bfloat16),
                pltpu.VMEM((own, span), jnp.bfloat16),
                dma((n_prompt // 4,)),
                pltpu.VMEM((HEAD, keys), jnp.bfloat16),
                pltpu.VMEM((keys, HEAD), jnp.bfloat16),
                pltpu.VMEM((2, UNIT * 128, keys), jnp.float32),
                pltpu.VMEM((UNIT * 128, 128), jnp.float32),
                pltpu.VMEM((4 * rows_peer, own), jnp.float32),
                pltpu.VMEM((own, 128), jnp.float32),
                pltpu.VMEM((8, own), jnp.float32),
                dma((4,)),
                dma((1,)),
                dma((1,)),
                dma((n_ctx // 2,)),
                dma((n_ctx // 2,)),
                dma((n_ctx // 2,)),
                dma((n_ctx // 2,)),
                dma((4,)),
                dma((4,)),
                dma((4,)),
                dma((4,)),
                dma((n_prompt,)),
                dma((n_prompt,)),
                dma((n_prompt,)),
                dma((n_prompt,)),
            ],
            compiler_params=pltpu.CompilerParams(collective_id=0, has_side_effects=True),
            name="gather_attend",
        )(prefix_qkv, rollout, order)
        step_rows = 512
        out, pout = pl.pallas_call(
            place_rows,
            grid=(own // step_rows,),
            out_shape=(
                jax.ShapeDtypeStruct((own, span), jnp.bfloat16),
                jax.ShapeDtypeStruct((block, span), jnp.bfloat16),
            ),
            in_specs=[
                pl.BlockSpec(memory_space=pltpu.SMEM),
                pl.BlockSpec((1, step_rows), lambda i: (0, i)),
                pl.BlockSpec((own, span), lambda i: (0, 0)),
                pl.BlockSpec((block, span), lambda i: (0, 0)),
            ],
            out_specs=(
                pl.BlockSpec((step_rows, span), lambda i: (i, 0)),
                pl.BlockSpec((block, span), lambda i: (0, 0)),
            ),
            name="place_rows",
        )(resp_len, order, tmp, ptmp)
        per = resp_len.shape[1]
        return pout[None], out.reshape(1, per, own // per, span)

    spec = P("prompt", "ctx", None)
    return jax.shard_map(
        body,
        mesh=mesh,
        in_specs=(spec, P("prompt", "ctx", None, None, None), spec, P("prompt", "ctx")),
        out_specs=(spec, P("prompt", "ctx", None, None)),
        check_vma=False,
    )
```

```python
import functools
import math

import jax
import jax.numpy as jnp
from jax import lax
from jax.experimental import pallas as pl
from jax.experimental.pallas import tpu as pltpu
from jax.sharding import PartitionSpec as P

HEAD = 128
MASKED = -1e30
MESH = pl.DeviceIdType.MESH
SCALE2 = HEAD ** (-0.5) * math.log2(math.e)
KEY_TILE = 512
UNIT = 2
NEAR = (1, 7, 2, 6)


def bit_flips(index, bits):
    return [(1 - 2 * lax.rem(lax.div(index, 1 << b), 2)) * (1 << b) for b in range(bits)]


def flipped(index, flips, mask):
    for b, step in enumerate(flips):
        if mask >> b & 1:
            index = index + step
    return index


def score_tile(queries, kt, s_ref, k0, top, extra):
    s = jnp.dot(queries, kt[:, k0 : k0 + KEY_TILE], preferred_element_type=jnp.float32)
    s = extra(k0, s)
    s_ref[:, k0 : k0 + KEY_TILE] = s
    for l0 in range(0, KEY_TILE, 128):
        part = s[:, l0 : l0 + 128]
        top = part if top is None else jnp.maximum(top, part)
    return top


def weigh_tile(va, s_ref, k0, top, carried):
    weights = jnp.exp2((s_ref[:, k0 : k0 + KEY_TILE] - top) * SCALE2)
    row_sum, total = carried
    for l0 in range(0, KEY_TILE, 128):
        part = weights[:, l0 : l0 + 128]
        row_sum = part if row_sum is None else row_sum + part
    part = jnp.dot(weights.astype(jnp.bfloat16), va[k0 : k0 + KEY_TILE, :], preferred_element_type=jnp.float32)
    return row_sum, part if total is None else total + part


def finish_rows(carried):
    row_sum, total = carried
    return (total / jnp.sum(row_sum, axis=-1, keepdims=True)).astype(jnp.bfloat16)


def attend_unit(queries, kt, va, s_ref, tiles, extra):
    top = None
    for k0 in tiles:
        top = score_tile(queries, kt, s_ref, k0, top, extra)
    top = jnp.max(top, axis=-1, keepdims=True)
    carried = None, None
    for k0 in tiles:
        carried = weigh_tile(va, s_ref, k0, top, carried)
    return (top,) + carried


def stack_heads(rows, h):
    return jnp.concatenate([rows[:, g * HEAD : (g + 1) * HEAD] for g in range(h, h + UNIT)], axis=0)


def gather_attend(
    n_prompt, n_ctx, heads,
    prefix_ref, rollout_ref, order_ref, pout_ref, rout_ref,
    pkv, rkv, rq, pq, pres, rres, out_sem, kt, va, s_ref, part_ref, bias_ref, gcol, grow,
    local_sem, part_send, part_recv, own_send, own_recv, fwd_send, fwd_recv, own_hop_send, own_hop_recv, fwd_hop_send, fwd_hop_recv,
    kv_send, kv_recv, q_send, q_recv,
):
    p = lax.axis_index("prompt")
    c = lax.axis_index("ctx")
    span = heads * HEAD
    width = span + 2 * HEAD
    peers = n_prompt.bit_length() - 1
    flips = bit_flips(p, peers)
    ring = n_ctx // 2
    z, side = lax.div(c, 2), lax.rem(c, 2)
    partner = c + 1 - 2 * side
    rows_peer = rkv.shape[1]
    block = pkv.shape[1]
    prefix_keys = n_ctx * block
    own_keys = n_prompt * rows_peer

    def along(step):
        return lax.rem(z + step, ring) * 2 + side

    barrier = pltpu.get_barrier_semaphore()
    for o in range(1, n_prompt):
        pl.semaphore_signal(barrier, inc=1, device_id=(flipped(p, flips, o), c), device_id_type=MESH)
    pl.semaphore_signal(barrier, inc=1, device_id=(p, partner), device_id_type=MESH)
    for k in NEAR:
        pl.semaphore_signal(barrier, inc=1, device_id=(p, along(k)), device_id_type=MESH)

    own_block = prefix_ref.at[0, :, pl.ds(span, 2 * HEAD)]
    local = [
        pltpu.make_async_copy(own_block, pkv.at[c], local_sem.at[0]),
        pltpu.make_async_copy(prefix_ref.at[0, :, pl.ds(0, span)], pq, local_sem.at[1]),
        pltpu.make_async_copy(rollout_ref.at[0, 0, p, :, pl.ds(span, 2 * HEAD)], rkv.at[p], local_sem.at[2]),
        pltpu.make_async_copy(rollout_ref.at[0, 0, p, :, pl.ds(0, span)], rq.at[p], local_sem.at[3]),
    ]
    for copy in local:
        copy.start()

    def to_partner(slot):
        return pltpu.make_async_remote_copy(
            own_block, pkv.at[slot], part_send.at[0], part_recv.at[0], device_id=(p, partner), device_id_type=MESH
        )

    def own_to(k, slot):
        return pltpu.make_async_remote_copy(
            own_block, pkv.at[slot], own_send.at[k], own_recv.at[k], device_id=(p, along(k)), device_id_type=MESH
        )

    def fwd_to(k, slot):
        return pltpu.make_async_remote_copy(
            pkv.at[partner], pkv.at[slot], fwd_send.at[k], fwd_recv.at[k], device_id=(p, along(k)), device_id_type=MESH
        )

    def hop_copies(own, arrived):
        slot = along if own else (lambda k: along(k) + 1 - 2 * side)
        send, recv = (own_hop_send, own_hop_recv) if own else (fwd_hop_send, fwd_hop_recv)
        half = block // 2
        low, high = pl.ds(0, half), pl.ds(half, half)
        before, after = pkv.at[slot(ring - 2)], pkv.at[slot(2)]
        ends = [before, before.at[low], after, after.at[high]]
        if arrived:
            ends = [pkv.at[slot(ring - 3)], pkv.at[slot(4), low], pkv.at[slot(3)], pkv.at[slot(4), high]]
        starts = [before, before.at[low], after, after.at[high]]
        return [
            pltpu.make_async_remote_copy(
                start, end, send.at[j], recv.at[j], device_id=(p, along(k)), device_id_type=MESH
            )
            for j, (start, end, k) in enumerate(zip(starts, ends, (1, 2, ring - 1, ring - 2)))
        ]

    def kv_to(o, slot):
        there = flipped(p, flips, o)
        return pltpu.make_async_remote_copy(
            rollout_ref.at[0, 0, there, :, pl.ds(span, 2 * HEAD)], rkv.at[slot],
            kv_send.at[o], kv_recv.at[o], device_id=(there, c), device_id_type=MESH,
        )

    def q_to(o, slot):
        there = flipped(p, flips, o)
        return pltpu.make_async_remote_copy(
            rollout_ref.at[0, 0, there, :, pl.ds(0, span)], rq.at[slot],
            q_send.at[o], q_recv.at[o], device_id=(there, c), device_id_type=MESH,
        )

    order = order_ref[...]
    place = lax.broadcasted_iota(jnp.int32, (128, own_keys), 1).astype(jnp.float32)
    for a0 in range(0, own_keys, 128):
        arrived = lax.broadcasted_iota(jnp.int32, (128, own_keys), 0) + a0
        at = jnp.sum(jnp.where(order == arrived, place, 0.0), axis=-1, keepdims=True)
        at = jnp.broadcast_to(at, (128, 128))
        gcol[a0 : a0 + 128, :] = at
        grow[:, a0 : a0 + 128] = at.T[:8]

    pl.semaphore_wait(barrier, n_prompt + len(NEAR))
    half = n_prompt // 2
    to_partner(c).start()
    for k in NEAR:
        own_to(k, c).start()
    for o in list(range(half, n_prompt)) + list(range(half // 2, half)) + list(range(1, half // 2)):
        kv_to(o, p).start()
    for o in range(1, n_prompt):
        q_to(o, p).start()

    for copy in local:
        copy.wait()

    side_keys = prefix_keys // 2
    far0 = side_keys + own_keys

    def take_prefix(slot, far):
        rows = pl.ds(pl.multiple_of(lax.div(slot, 2) * block + (far0 if far else 0), block), block)
        got = pkv[slot]
        kt[:, rows] = got[:, :HEAD].T
        va[rows, :] = got[:, HEAD:]

    def other(k):
        return along(k) + 1 - 2 * side

    take_prefix(c, False)
    to_partner(partner).wait_recv()
    for k in NEAR:
        fwd_to(k, partner).start()
    own_hops = hop_copies(True, False)
    own_to(2, along(ring - 2)).wait_recv()
    own_hops[0].start()
    own_hops[1].start()
    own_to(ring - 2, along(2)).wait_recv()
    own_hops[2].start()
    own_hops[3].start()
    take_prefix(partner, True)
    take_prefix(along(2), False)
    take_prefix(along(ring - 2), False)
    for k in (1, ring - 1):
        own_to(k, along(ring - k)).wait_recv()
        take_prefix(along(ring - k), False)
    for o in range(1, n_prompt):
        kv_to(o, flipped(p, flips, o)).wait_recv()
    for a0 in range(0, own_keys, 128):
        got = rkv[a0 // rows_peer : (a0 + 128) // rows_peer].reshape(128, 2 * HEAD)
        at = side_keys + a0
        kt[:, at : at + 128] = got[:, :HEAD].T
        va[at : at + 128, :] = got[:, HEAD:]
    for copy in hop_copies(True, True):
        copy.wait_recv()
    for k in (3, 4, 5):
        take_prefix(along(k), False)

    quad = lax.div(p, 4)
    chunk_rows = 4 * rows_peer
    chunks = n_prompt // 4
    keys = prefix_keys + own_keys
    early = chunks // 2
    units = heads // UNIT
    fwd_hops = hop_copies(False, False)

    def base_of(i):
        base = 0
        for b in range(peers - 2):
            base = base + lax.rem(lax.div(quad, 1 << b) + lax.div(i, 1 << b), 2) * (1 << b)
        return base

    def get_chunk(i):
        base = base_of(i)
        for k in range(4):
            @pl.when(i * 4 + k > 0)
            def _():
                from_peer = base * 4 + flipped(lax.rem(p, 4), flips[:2], k)
                pltpu.make_async_remote_copy(
                    rollout_ref.at[0, 0, from_peer, :, pl.ds(0, span)], rq.at[from_peer],
                    q_send.at[i * 4 + k], q_recv.at[i * 4 + k], device_id=(from_peer, c), device_id_type=MESH,
                ).wait_recv()
        mine = gcol[pl.ds(pl.multiple_of(base * chunk_rows, chunk_rows), chunk_rows), :]
        first = jnp.where(mine >= own_keys // 2, float(own_keys // 2), 0.0)
        for k0 in range(0, own_keys, 128):
            seen = (grow[0:1, k0 : k0 + 128] <= mine) & (grow[0:1, k0 : k0 + 128] >= first)
            bias_ref[:, k0 : k0 + 128] = jnp.where(seen, 0.0, MASKED)

    def masked(k0, s):
        if k0 < side_keys or k0 >= far0:
            return s
        bias = bias_ref[:, k0 - side_keys : k0 - side_keys + KEY_TILE]
        return s + jnp.concatenate([bias] * UNIT, axis=0)

    def queries_of(i, u):
        return stack_heads(rq[pl.ds(base_of(i) * 4, 4)].reshape(chunk_rows, span), u * UNIT)

    def put_rows(i, u, out):
        rows = pl.ds(pl.multiple_of(base_of(i) * chunk_rows, chunk_rows), chunk_rows)
        for g in range(UNIT):
            h = u * UNIT + g
            rres[rows, h * HEAD : (h + 1) * HEAD] = out[g * chunk_rows : (g + 1) * chunk_rows]

    def leave(i):
        rows = pl.ds(pl.multiple_of(base_of(i) * chunk_rows, chunk_rows), chunk_rows)
        return pltpu.make_async_copy(rres.at[rows], rout_ref.at[rows], out_sem.at[i])

    @pl.loop(0, early)
    def _(i):
        @pl.when(i == early // 2)
        def _():
            fwd_to(2, other(ring - 2)).wait_recv()
            fwd_hops[0].start()
            fwd_hops[1].start()
            fwd_to(ring - 2, other(2)).wait_recv()
            fwd_hops[2].start()
            fwd_hops[3].start()

        get_chunk(i)
        for u in range(units):
            top, row_sum, total = attend_unit(
                queries_of(i, u), kt, va, s_ref.at[u % 2], range(0, far0, KEY_TILE), masked
            )
            at = i * units + u
            part_ref[at, 0] = jnp.broadcast_to(top, row_sum.shape)
            part_ref[at, 1] = row_sum
            part_ref[at, 2] = total

    take_prefix(other(2), True)
    take_prefix(other(ring - 2), True)
    for k in (1, ring - 1):
        fwd_to(k, other(ring - k)).wait_recv()
        take_prefix(other(ring - k), True)
    for copy in hop_copies(False, True):
        copy.wait_recv()
    for k in (3, 4, 5):
        take_prefix(other(k), True)

    @pl.loop(0, early)
    def _(i):
        for u in range(units):
            top, row_sum, total = attend_unit(
                queries_of(i, u), kt, va, s_ref.at[u % 2], range(far0, keys, KEY_TILE), masked
            )
            at = i * units + u
            before = part_ref[at, 0]
            joint = jnp.maximum(before, top)
            keep = jnp.exp2((before - joint) * SCALE2)
            add = jnp.exp2((top - joint) * SCALE2)
            put_rows(i, u, finish_rows((part_ref[at, 1] * keep + row_sum * add, part_ref[at, 2] * keep + total * add)))
        leave(i).start()

    row = c * block + lax.rem(lax.broadcasted_iota(jnp.int32, (UNIT * block, KEY_TILE), 0), block)
    lane = lax.broadcasted_iota(jnp.int32, (UNIT * block, KEY_TILE), 1)
    lane = lax.div(lane, block) * (2 * block) + lax.rem(lane, block)

    def causal(k0, s):
        start = 2 * (k0 - far0) + (1 - side) * block if k0 >= far0 else 2 * k0 + side * block
        return jnp.where(lane + start <= row, s, MASKED)

    prefix_tiles = [*range(0, side_keys, KEY_TILE), *range(far0, keys, KEY_TILE)]
    for u in range(units):
        top, row_sum, total = attend_unit(stack_heads(pq, u * UNIT), kt, va, s_ref.at[u % 2], prefix_tiles, causal)
        out = finish_rows((row_sum, total))
        for g in range(UNIT):
            h = u * UNIT + g
            pres[:, h * HEAD : (h + 1) * HEAD] = out[g * block : (g + 1) * block]
    pout = pltpu.make_async_copy(pres, pout_ref, local_sem.at[0])
    pout.start()

    @pl.loop(early, chunks)
    def _(i):
        get_chunk(i)
        for u in range(units):
            top, row_sum, total = attend_unit(
                queries_of(i, u), kt, va, s_ref.at[u % 2], range(0, keys, KEY_TILE), masked
            )
            put_rows(i, u, finish_rows((row_sum, total)))
        leave(i).start()

    pout.wait()
    for i in range(chunks):
        leave(i).wait()
    to_partner(c).wait_send()
    for k in NEAR:
        own_to(k, c).wait_send()
        fwd_to(k, partner).wait_send()
    for copy in own_hops + fwd_hops:
        copy.wait_send()
    for o in range(1, n_prompt):
        kv_to(o, p).wait_send()
        q_to(o, p).wait_send()


def place_rows(len_ref, order_ref, tmp_ref, ptmp_ref, rout_ref, pout_ref):
    step = pl.program_id(0)
    rows = rout_ref.shape[0]
    total = tmp_ref.shape[0]
    per_resp = total // len_ref.shape[1] // rows

    @pl.when(step == 0)
    def _():
        pout_ref[...] = ptmp_ref[...]

    limit = len_ref[0, lax.div(step, per_resp)] - lax.rem(step, per_resp) * rows
    order = jnp.broadcast_to(order_ref[...], (128, rows)).T
    live = lax.broadcasted_iota(jnp.int32, (rows, 128), 0) < limit
    order = jnp.where(live, order, -1)
    lane = lax.broadcasted_iota(jnp.int32, (rows, 128), 1)
    pick = jnp.concatenate(
        [jnp.where(order == lane + a0, 1.0, 0.0).astype(jnp.bfloat16) for a0 in range(0, total, 128)], axis=1
    )
    rout_ref[...] = jnp.dot(pick, tmp_ref[...], preferred_element_type=jnp.float32).astype(jnp.bfloat16)


def solution(mesh):
    n_prompt, n_ctx = mesh.shape["prompt"], mesh.shape["ctx"]

    def body(prefix_qkv, rollout, arrival_order, resp_len):
        block, width = prefix_qkv.shape[1:]
        rows_peer = rollout.shape[3]
        span = width - 2 * HEAD
        heads = span // HEAD
        own = n_prompt * rows_peer
        keys = n_ctx * block + own
        order = arrival_order.reshape(1, own)
        dma = pltpu.SemaphoreType.DMA
        any_spec = pl.BlockSpec(memory_space=pl.ANY)
        vmem_spec = pl.BlockSpec(memory_space=pltpu.VMEM)
        ptmp, tmp = pl.pallas_call(
            functools.partial(gather_attend, n_prompt, n_ctx, heads),
            out_shape=(
                jax.ShapeDtypeStruct((block, span), jnp.bfloat16),
                jax.ShapeDtypeStruct((own, span), jnp.bfloat16),
            ),
            in_specs=[any_spec, any_spec, vmem_spec],
            out_specs=(any_spec, any_spec),
            scratch_shapes=[
                pltpu.VMEM((n_ctx, block, 2 * HEAD), jnp.bfloat16),
                pltpu.VMEM((n_prompt, rows_peer, 2 * HEAD), jnp.bfloat16),
                pltpu.VMEM((n_prompt, rows_peer, span), jnp.bfloat16),
                pltpu.VMEM((block, span), jnp.bfloat16),
                pltpu.VMEM((block, span), jnp.bfloat16),
                pltpu.VMEM((own, span), jnp.bfloat16),
                dma((n_prompt // 4,)),
                pltpu.VMEM((HEAD, keys), jnp.bfloat16),
                pltpu.VMEM((keys, HEAD), jnp.bfloat16),
                pltpu.VMEM((2, UNIT * 128, keys), jnp.float32),
                pltpu.VMEM((n_prompt // 8 * heads // UNIT, 3, UNIT * 4 * rows_peer, HEAD), jnp.float32),
                pltpu.VMEM((4 * rows_peer, own), jnp.float32),
                pltpu.VMEM((own, 128), jnp.float32),
                pltpu.VMEM((8, own), jnp.float32),
                dma((4,)),
                dma((1,)),
                dma((1,)),
                dma((n_ctx // 2,)),
                dma((n_ctx // 2,)),
                dma((n_ctx // 2,)),
                dma((n_ctx // 2,)),
                dma((4,)),
                dma((4,)),
                dma((4,)),
                dma((4,)),
                dma((n_prompt,)),
                dma((n_prompt,)),
                dma((n_prompt,)),
                dma((n_prompt,)),
            ],
            compiler_params=pltpu.CompilerParams(collective_id=0, has_side_effects=True),
            name="gather_attend",
        )(prefix_qkv, rollout, order)
        step_rows = 512
        out, pout = pl.pallas_call(
            place_rows,
            grid=(own // step_rows,),
            out_shape=(
                jax.ShapeDtypeStruct((own, span), jnp.bfloat16),
                jax.ShapeDtypeStruct((block, span), jnp.bfloat16),
            ),
            in_specs=[
                pl.BlockSpec(memory_space=pltpu.SMEM),
                pl.BlockSpec((1, step_rows), lambda i: (0, i)),
                pl.BlockSpec((own, span), lambda i: (0, 0)),
                pl.BlockSpec((block, span), lambda i: (0, 0)),
            ],
            out_specs=(
                pl.BlockSpec((step_rows, span), lambda i: (i, 0)),
                pl.BlockSpec((block, span), lambda i: (0, 0)),
            ),
            name="place_rows",
        )(resp_len, order, tmp, ptmp)
        per = resp_len.shape[1]
        return pout[None], out.reshape(1, per, own // per, span)

    spec = P("prompt", "ctx", None)
    return jax.shard_map(
        body,
        mesh=mesh,
        in_specs=(spec, P("prompt", "ctx", None, None, None), spec, P("prompt", "ctx")),
        out_specs=(spec, P("prompt", "ctx", None, None)),
        check_vma=False,
    )
```

```python
import functools
import math

import jax
import jax.numpy as jnp
from jax import lax
from jax.experimental import pallas as pl
from jax.experimental.pallas import tpu as pltpu
from jax.sharding import PartitionSpec as P

HEAD = 128
MASKED = -1e30
MESH = pl.DeviceIdType.MESH
SCALE2 = HEAD ** (-0.5) * math.log2(math.e)
KEY_TILE = 512
UNIT = 2
NEAR = (1, 7, 2, 6)


def bit_flips(index, bits):
    return [(1 - 2 * lax.rem(lax.div(index, 1 << b), 2)) * (1 << b) for b in range(bits)]


def flipped(index, flips, mask):
    for b, step in enumerate(flips):
        if mask >> b & 1:
            index = index + step
    return index


def score_tile(queries, kt, s_ref, k0, top, extra):
    s = jnp.dot(queries, kt[:, k0 : k0 + KEY_TILE], preferred_element_type=jnp.float32)
    s = extra(k0, s)
    s_ref[:, k0 : k0 + KEY_TILE] = s
    for l0 in range(0, KEY_TILE, 128):
        part = s[:, l0 : l0 + 128]
        top = part if top is None else jnp.maximum(top, part)
    return top


def weigh_tile(va, s_ref, k0, top, carried):
    weights = jnp.exp2((s_ref[:, k0 : k0 + KEY_TILE] - top) * SCALE2)
    row_sum, total = carried
    for l0 in range(0, KEY_TILE, 128):
        part = weights[:, l0 : l0 + 128]
        row_sum = part if row_sum is None else row_sum + part
    part = jnp.dot(weights.astype(jnp.bfloat16), va[k0 : k0 + KEY_TILE, :], preferred_element_type=jnp.float32)
    return row_sum, part if total is None else total + part


def finish_rows(carried):
    row_sum, total = carried
    return (total / jnp.sum(row_sum, axis=-1, keepdims=True)).astype(jnp.bfloat16)


def attend_unit(queries, kt, va, s_ref, tiles, extra):
    top = None
    for k0 in tiles:
        top = score_tile(queries, kt, s_ref, k0, top, extra)
    top = jnp.max(top, axis=-1, keepdims=True)
    carried = None, None
    for k0 in tiles:
        carried = weigh_tile(va, s_ref, k0, top, carried)
    return (top,) + carried


def stack_heads(rows, h):
    return jnp.concatenate([rows[:, g * HEAD : (g + 1) * HEAD] for g in range(h, h + UNIT)], axis=0)


def gather_attend(
    n_prompt, n_ctx, heads,
    prefix_ref, rollout_ref, order_ref, pout_ref, rout_ref,
    pkv, rkv, rq, pq, pres, rres, out_sem, kt, va, s_ref, part_ref, bias_ref, gcol, grow,
    local_sem, part_send, part_recv, own_send, own_recv, fwd_send, fwd_recv, own_hop_send, own_hop_recv, fwd_hop_send, fwd_hop_recv,
    kv_send, kv_recv, q_send, q_recv,
):
    p = lax.axis_index("prompt")
    c = lax.axis_index("ctx")
    span = heads * HEAD
    width = span + 2 * HEAD
    peers = n_prompt.bit_length() - 1
    flips = bit_flips(p, peers)
    ring = n_ctx // 2
    z, side = lax.div(c, 2), lax.rem(c, 2)
    partner = c + 1 - 2 * side
    rows_peer = rkv.shape[1]
    block = pkv.shape[1]
    prefix_keys = n_ctx * block
    own_keys = n_prompt * rows_peer

    def along(step):
        return lax.rem(z + step, ring) * 2 + side

    barrier = pltpu.get_barrier_semaphore()
    for o in range(1, n_prompt):
        pl.semaphore_signal(barrier, inc=1, device_id=(flipped(p, flips, o), c), device_id_type=MESH)
    pl.semaphore_signal(barrier, inc=1, device_id=(p, partner), device_id_type=MESH)
    for k in NEAR:
        pl.semaphore_signal(barrier, inc=1, device_id=(p, along(k)), device_id_type=MESH)

    own_block = prefix_ref.at[0, :, pl.ds(span, 2 * HEAD)]
    local = [
        pltpu.make_async_copy(own_block, pkv.at[c], local_sem.at[0]),
        pltpu.make_async_copy(prefix_ref.at[0, :, pl.ds(0, span)], pq, local_sem.at[1]),
        pltpu.make_async_copy(rollout_ref.at[0, 0, p, :, pl.ds(span, 2 * HEAD)], rkv.at[p], local_sem.at[2]),
        pltpu.make_async_copy(rollout_ref.at[0, 0, p, :, pl.ds(0, span)], rq.at[lax.div(p, 2), lax.rem(p, 2)], local_sem.at[3]),
    ]
    for copy in local:
        copy.start()

    def to_partner(slot):
        return pltpu.make_async_remote_copy(
            own_block, pkv.at[slot], part_send.at[0], part_recv.at[0], device_id=(p, partner), device_id_type=MESH
        )

    def own_to(k, slot):
        return pltpu.make_async_remote_copy(
            own_block, pkv.at[slot], own_send.at[k], own_recv.at[k], device_id=(p, along(k)), device_id_type=MESH
        )

    def fwd_to(k, slot):
        return pltpu.make_async_remote_copy(
            pkv.at[partner], pkv.at[slot], fwd_send.at[k], fwd_recv.at[k], device_id=(p, along(k)), device_id_type=MESH
        )

    def hop_copies(own, arrived):
        slot = along if own else (lambda k: along(k) + 1 - 2 * side)
        send, recv = (own_hop_send, own_hop_recv) if own else (fwd_hop_send, fwd_hop_recv)
        half = block // 2
        low, high = pl.ds(0, half), pl.ds(half, half)
        before, after = pkv.at[slot(ring - 2)], pkv.at[slot(2)]
        ends = [before, before.at[low], after, after.at[high]]
        if arrived:
            ends = [pkv.at[slot(ring - 3)], pkv.at[slot(4), low], pkv.at[slot(3)], pkv.at[slot(4), high]]
        starts = [before, before.at[low], after, after.at[high]]
        return [
            pltpu.make_async_remote_copy(
                start, end, send.at[j], recv.at[j], device_id=(p, along(k)), device_id_type=MESH
            )
            for j, (start, end, k) in enumerate(zip(starts, ends, (1, 2, ring - 1, ring - 2)))
        ]

    def kv_to(o, slot):
        there = flipped(p, flips, o)
        return pltpu.make_async_remote_copy(
            rollout_ref.at[0, 0, there, :, pl.ds(span, 2 * HEAD)], rkv.at[slot],
            kv_send.at[o], kv_recv.at[o], device_id=(there, c), device_id_type=MESH,
        )

    def q_to(o, slot):
        there = flipped(p, flips, o)
        return pltpu.make_async_remote_copy(
            rollout_ref.at[0, 0, there, :, pl.ds(0, span)], rq.at[lax.div(slot, 2), lax.rem(slot, 2)],
            q_send.at[o], q_recv.at[o], device_id=(there, c), device_id_type=MESH,
        )

    order = order_ref[...]
    place = lax.broadcasted_iota(jnp.int32, (128, own_keys), 1).astype(jnp.float32)
    for a0 in range(0, own_keys, 128):
        arrived = lax.broadcasted_iota(jnp.int32, (128, own_keys), 0) + a0
        at = jnp.sum(jnp.where(order == arrived, place, 0.0), axis=-1, keepdims=True)
        at = jnp.broadcast_to(at, (128, 128))
        pair = 2 * rows_peer
        gcol[a0 // pair : (a0 + 128) // pair] = at.reshape(128 // pair, 2, rows_peer, 128)
        grow[:, a0 : a0 + 128] = at.T[:8]

    pl.semaphore_wait(barrier, n_prompt + len(NEAR))
    half = n_prompt // 2
    to_partner(c).start()
    for k in NEAR:
        own_to(k, c).start()
    for o in list(range(half, n_prompt)) + list(range(half // 2, half)) + list(range(1, half // 2)):
        kv_to(o, p).start()
    for o in sorted(range(1, n_prompt), key=lambda o: (o // 8, o % 2, o)):
        q_to(o, p).start()

    for copy in local:
        copy.wait()

    side_keys = prefix_keys // 2
    far0 = side_keys + own_keys

    def take_prefix(slot, far):
        rows = pl.ds(pl.multiple_of(lax.div(slot, 2) * block + (far0 if far else 0), block), block)
        got = pkv[slot]
        kt[:, rows] = got[:, :HEAD].T
        va[rows, :] = got[:, HEAD:]

    def other(k):
        return along(k) + 1 - 2 * side

    take_prefix(c, False)
    to_partner(partner).wait_recv()
    for k in NEAR:
        fwd_to(k, partner).start()
    own_hops = hop_copies(True, False)
    own_to(2, along(ring - 2)).wait_recv()
    own_hops[0].start()
    own_hops[1].start()
    own_to(ring - 2, along(2)).wait_recv()
    own_hops[2].start()
    own_hops[3].start()
    take_prefix(partner, True)
    take_prefix(along(2), False)
    take_prefix(along(ring - 2), False)
    for k in (1, ring - 1):
        own_to(k, along(ring - k)).wait_recv()
        take_prefix(along(ring - k), False)
    for o in range(1, n_prompt):
        kv_to(o, flipped(p, flips, o)).wait_recv()
    for a0 in range(0, own_keys, 128):
        got = rkv[a0 // rows_peer : (a0 + 128) // rows_peer].reshape(128, 2 * HEAD)
        at = side_keys + a0
        kt[:, at : at + 128] = got[:, :HEAD].T
        va[at : at + 128, :] = got[:, HEAD:]
    for copy in hop_copies(True, True):
        copy.wait_recv()
    for k in (3, 4, 5):
        take_prefix(along(k), False)

    chunk_rows = 4 * rows_peer
    chunks = n_prompt // 4
    keys = prefix_keys + own_keys
    early = chunks // 2
    units = heads // UNIT
    fwd_hops = hop_copies(False, False)

    def line_of(i):
        line = 0
        for b in range(peers - 3):
            line = line + lax.rem(lax.div(p, 8 << b) + lax.div(i, 2 << b), 2) * (1 << b)
        return pl.ds(line * 4, 4), lax.rem(p + i, 2), line

    def get_chunk(i):
        pairs, core, line = line_of(i)
        x_part = lax.rem(p, 8) - lax.rem(p, 2)
        for k in range(4):
            @pl.when(i * 4 + k > 0)
            def _():
                from_peer = line * 8 + flipped(x_part, flips[1:3], k) + core
                at = lax.div(i, 2) * 8 + k * 2 + lax.rem(i, 2)
                pltpu.make_async_remote_copy(
                    rollout_ref.at[0, 0, from_peer, :, pl.ds(0, span)], rq.at[lax.div(from_peer, 2), core],
                    q_send.at[at], q_recv.at[at], device_id=(from_peer, c), device_id_type=MESH,
                ).wait_recv()
        mine = gcol[pairs, core].reshape(chunk_rows, 128)
        first = jnp.where(mine >= own_keys // 2, float(own_keys // 2), 0.0)
        for k0 in range(0, own_keys, 128):
            seen = (grow[0:1, k0 : k0 + 128] <= mine) & (grow[0:1, k0 : k0 + 128] >= first)
            bias_ref[:, k0 : k0 + 128] = jnp.where(seen, 0.0, MASKED)

    def masked(k0, s):
        if k0 < side_keys or k0 >= far0:
            return s
        bias = bias_ref[:, k0 - side_keys : k0 - side_keys + KEY_TILE]
        return s + jnp.concatenate([bias] * UNIT, axis=0)

    def queries_of(i, u):
        pairs, core, _ = line_of(i)
        return stack_heads(rq[pairs, core].reshape(chunk_rows, span), u * UNIT)

    def put_rows(i, u, out):
        pairs, core, _ = line_of(i)
        for g in range(UNIT):
            h = u * UNIT + g
            rows = out[g * chunk_rows : (g + 1) * chunk_rows].reshape(4, rows_peer, HEAD)
            rres[pairs, core, :, h * HEAD : (h + 1) * HEAD] = rows

    def leave(i):
        pairs, core, _ = line_of(i)
        return pltpu.make_async_copy(rres.at[pairs, core], rout_ref.at[pairs, core], out_sem.at[i])

    @pl.loop(0, early)
    def _(i):
        @pl.when(i == early // 2)
        def _():
            fwd_to(2, other(ring - 2)).wait_recv()
            fwd_hops[0].start()
            fwd_hops[1].start()
            fwd_to(ring - 2, other(2)).wait_recv()
            fwd_hops[2].start()
            fwd_hops[3].start()

        get_chunk(i)
        for u in range(units):
            top, row_sum, total = attend_unit(
                queries_of(i, u), kt, va, s_ref.at[u % 2], range(0, far0, KEY_TILE), masked
            )
            at = i * units + u
            part_ref[at, 0] = jnp.broadcast_to(top, row_sum.shape)
            part_ref[at, 1] = row_sum
            part_ref[at, 2] = total

    take_prefix(other(2), True)
    take_prefix(other(ring - 2), True)
    for k in (1, ring - 1):
        fwd_to(k, other(ring - k)).wait_recv()
        take_prefix(other(ring - k), True)
    for copy in hop_copies(False, True):
        copy.wait_recv()
    for k in (3, 4, 5):
        take_prefix(other(k), True)

    @pl.loop(0, early)
    def _(i):
        for u in range(units):
            top, row_sum, total = attend_unit(
                queries_of(i, u), kt, va, s_ref.at[u % 2], range(far0, keys, KEY_TILE), masked
            )
            at = i * units + u
            before = part_ref[at, 0]
            joint = jnp.maximum(before, top)
            keep = jnp.exp2((before - joint) * SCALE2)
            add = jnp.exp2((top - joint) * SCALE2)
            put_rows(i, u, finish_rows((part_ref[at, 1] * keep + row_sum * add, part_ref[at, 2] * keep + total * add)))
        leave(i).start()

    row = c * block + lax.rem(lax.broadcasted_iota(jnp.int32, (UNIT * block, KEY_TILE), 0), block)
    lane = lax.broadcasted_iota(jnp.int32, (UNIT * block, KEY_TILE), 1)
    lane = lax.div(lane, block) * (2 * block) + lax.rem(lane, block)

    def causal(k0, s):
        start = 2 * (k0 - far0) + (1 - side) * block if k0 >= far0 else 2 * k0 + side * block
        return jnp.where(lane + start <= row, s, MASKED)

    prefix_tiles = [*range(0, side_keys, KEY_TILE), *range(far0, keys, KEY_TILE)]
    for u in range(units):
        top, row_sum, total = attend_unit(stack_heads(pq, u * UNIT), kt, va, s_ref.at[u % 2], prefix_tiles, causal)
        out = finish_rows((row_sum, total))
        for g in range(UNIT):
            h = u * UNIT + g
            pres[:, h * HEAD : (h + 1) * HEAD] = out[g * block : (g + 1) * block]
    pout = pltpu.make_async_copy(pres, pout_ref, local_sem.at[0])
    pout.start()

    @pl.loop(early, chunks)
    def _(i):
        get_chunk(i)
        for u in range(units):
            top, row_sum, total = attend_unit(
                queries_of(i, u), kt, va, s_ref.at[u % 2], range(0, keys, KEY_TILE), masked
            )
            put_rows(i, u, finish_rows((row_sum, total)))
        leave(i).start()

    pout.wait()
    for i in range(chunks):
        leave(i).wait()
    to_partner(c).wait_send()
    for k in NEAR:
        own_to(k, c).wait_send()
        fwd_to(k, partner).wait_send()
    for copy in own_hops + fwd_hops:
        copy.wait_send()
    for o in range(1, n_prompt):
        kv_to(o, p).wait_send()
        q_to(o, p).wait_send()


def place_rows(len_ref, order_ref, tmp_ref, ptmp_ref, rout_ref, pout_ref):
    step = pl.program_id(0)
    rows = rout_ref.shape[0]
    total = tmp_ref.shape[0]
    per_resp = total // len_ref.shape[1] // rows

    @pl.when(step == 0)
    def _():
        pout_ref[...] = ptmp_ref[...]

    limit = len_ref[0, lax.div(step, per_resp)] - lax.rem(step, per_resp) * rows
    order = jnp.broadcast_to(order_ref[...], (128, rows)).T
    live = lax.broadcasted_iota(jnp.int32, (rows, 128), 0) < limit
    order = jnp.where(live, order, -1)
    lane = lax.broadcasted_iota(jnp.int32, (rows, 128), 1)
    pick = jnp.concatenate(
        [jnp.where(order == lane + a0, 1.0, 0.0).astype(jnp.bfloat16) for a0 in range(0, total, 128)], axis=1
    )
    rout_ref[...] = jnp.dot(pick, tmp_ref[...], preferred_element_type=jnp.float32).astype(jnp.bfloat16)


def solution(mesh):
    n_prompt, n_ctx = mesh.shape["prompt"], mesh.shape["ctx"]

    def body(prefix_qkv, rollout, arrival_order, resp_len):
        block, width = prefix_qkv.shape[1:]
        rows_peer = rollout.shape[3]
        span = width - 2 * HEAD
        heads = span // HEAD
        own = n_prompt * rows_peer
        keys = n_ctx * block + own
        order = arrival_order.reshape(1, own)
        dma = pltpu.SemaphoreType.DMA
        any_spec = pl.BlockSpec(memory_space=pl.ANY)
        vmem_spec = pl.BlockSpec(memory_space=pltpu.VMEM)
        ptmp, tmp = pl.pallas_call(
            functools.partial(gather_attend, n_prompt, n_ctx, heads),
            out_shape=(
                jax.ShapeDtypeStruct((block, span), jnp.bfloat16),
                jax.ShapeDtypeStruct((n_prompt // 2, 2, rows_peer, span), jnp.bfloat16),
            ),
            in_specs=[any_spec, any_spec, vmem_spec],
            out_specs=(any_spec, any_spec),
            scratch_shapes=[
                pltpu.VMEM((n_ctx, block, 2 * HEAD), jnp.bfloat16),
                pltpu.VMEM((n_prompt, rows_peer, 2 * HEAD), jnp.bfloat16),
                pltpu.VMEM((n_prompt // 2, 2, rows_peer, span), jnp.bfloat16),
                pltpu.VMEM((block, span), jnp.bfloat16),
                pltpu.VMEM((block, span), jnp.bfloat16),
                pltpu.VMEM((n_prompt // 2, 2, rows_peer, span), jnp.bfloat16),
                dma((n_prompt // 4,)),
                pltpu.VMEM((HEAD, keys), jnp.bfloat16),
                pltpu.VMEM((keys, HEAD), jnp.bfloat16),
                pltpu.VMEM((2, UNIT * 128, keys), jnp.float32),
                pltpu.VMEM((n_prompt // 8 * heads // UNIT, 3, UNIT * 4 * rows_peer, HEAD), jnp.float32),
                pltpu.VMEM((4 * rows_peer, own), jnp.float32),
                pltpu.VMEM((n_prompt // 2, 2, rows_peer, 128), jnp.float32),
                pltpu.VMEM((8, own), jnp.float32),
                dma((4,)),
                dma((1,)),
                dma((1,)),
                dma((n_ctx // 2,)),
                dma((n_ctx // 2,)),
                dma((n_ctx // 2,)),
                dma((n_ctx // 2,)),
                dma((4,)),
                dma((4,)),
                dma((4,)),
                dma((4,)),
                dma((n_prompt,)),
                dma((n_prompt,)),
                dma((n_prompt,)),
                dma((n_prompt,)),
            ],
            compiler_params=pltpu.CompilerParams(collective_id=0, has_side_effects=True),
            name="gather_attend",
        )(prefix_qkv, rollout, order)
        step_rows = 512
        out, pout = pl.pallas_call(
            place_rows,
            grid=(own // step_rows,),
            out_shape=(
                jax.ShapeDtypeStruct((own, span), jnp.bfloat16),
                jax.ShapeDtypeStruct((block, span), jnp.bfloat16),
            ),
            in_specs=[
                pl.BlockSpec(memory_space=pltpu.SMEM),
                pl.BlockSpec((1, step_rows), lambda i: (0, i)),
                pl.BlockSpec((own, span), lambda i: (0, 0)),
                pl.BlockSpec((block, span), lambda i: (0, 0)),
            ],
            out_specs=(
                pl.BlockSpec((step_rows, span), lambda i: (i, 0)),
                pl.BlockSpec((block, span), lambda i: (0, 0)),
            ),
            name="place_rows",
        )(resp_len, order, tmp.reshape(own, span), ptmp)
        per = resp_len.shape[1]
        return pout[None], out.reshape(1, per, own // per, span)

    spec = P("prompt", "ctx", None)
    return jax.shard_map(
        body,
        mesh=mesh,
        in_specs=(spec, P("prompt", "ctx", None, None, None), spec, P("prompt", "ctx")),
        out_specs=(spec, P("prompt", "ctx", None, None)),
        check_vma=False,
    )
```
